512 devices in a mesh: brow: 32 (over z_lo, y, core), bcol: 16 (over z_hi, x).
Axes of the slice: x: 4, y: 8, z: 8 (z_hi: 4, z_lo: 2; z = z_hi * 2 + z_lo), core: 2. Of those that a mesh axis runs over, the one named last changes fastest.
Arguments:
- vectors: bfloat16 [8, 1048576], P(None, ('brow', 'bcol')), may hold values from -6 to 6
- tiles: bfloat16 [98304, 4096], P(('brow', 'bcol')), may hold values from -0.29882812 to 0.29882812
- tile_rows: int32 [98304], P(('brow', 'bcol')), may hold values from 0 to 511
- tile_cols: int32 [98304], P(('brow', 'bcol')), may hold values from 0 to 1023
- counts: int32 [32, 16], P('brow', 'bcol'), may hold values from 64 to 192, as said below
Outputs:
- product: float32 [8, 1048576], P(None, ('brow', 'bcol'))
The draws below stay inside these ranges and needn't reach their ends.
Inputs may be any that keep to these rules, and one draw needn't show every extreme that they name: `counts`: some grid block uses all 192 slots in every draw; every block uses at least a third of them.
All inputs are finite; a program needn't handle non-finite values.
Results may differ from the reference program's by a relative error of at most 0.0003.
Values may be sent and summed in bfloat16 or wider, within the bound.
A program may use at most 64 MiB of HBM per device.

```python
import jax
import jax.numpy as jnp
from jax import lax

PIECE = 2048
TMAX = 192
VECS = 8
TILE = 64
DIM = 1048576
TILES = 98304
N_BROW = 32
N_BCOL = 16


def draw_counts(key, part):
    first_key, second_key = jax.random.split(jax.random.fold_in(key, 17))
    values = jax.random.randint(first_key, (N_BROW * N_BCOL,), TMAX // 3, TMAX + 1)
    picked = jax.random.randint(second_key, (), 0, N_BROW * N_BCOL)
    values = values.at[picked].set(TMAX)
    return values.reshape(N_BROW, N_BCOL).astype(jnp.int32)


def set_ends(drawn, rng, least, largest):
    dims = drawn.shape
    place = [jax.random.randint(jax.random.fold_in(rng, axis), (), 0, dims[axis]) for axis in range(len(dims))]
    drawn = drawn.at[tuple(place)].set(least)
    longest = dims.index(max(dims))
    place[longest] = (place[longest] + 1) % dims[longest]
    return drawn.at[tuple(place)].set(largest)


def block_scale(own_key, dims, cuts, low, largest):
    level, own = 1.0, jax.random.fold_in(own_key, 6)
    for position, shards_of in cuts:
        heights = jnp.exp(jax.random.uniform(jax.random.fold_in(own, position), (shards_of,), jnp.float32, low / len(cuts), largest / len(cuts)))
        level = level * jnp.repeat(heights, dims[position] // shards_of).reshape([-1 if axis == position else 1 for axis in range(len(dims))])
    return level


def gaussian(own_key, shape, width, limit, shards=(), held_as=jnp.bfloat16):
    factor_of = block_scale(own_key, shape, shards, -0.22, 0.18) if shards else 1.0
    values = jax.random.normal(own_key, shape, jnp.float32) * width * factor_of
    return jnp.minimum(jnp.maximum(values, -limit), limit).astype(held_as)


def setup_inputs(seed: int = 0) -> dict:
    key_of = jax.random.split(jax.random.key(seed), 6)
    vectors = gaussian(key_of[0], (VECS, DIM), 1.0, 6.0, ((1, 512),))
    tiles = gaussian(key_of[1], (TILES, TILE * TILE), 0.05, 0.29882812, ((0, 512),))
    tile_rows = set_ends(jax.random.randint(key_of[2], (TILES,), 0, PIECE * N_BCOL // TILE), jax.random.fold_in(key_of[2], 1), 0, (PIECE * N_BCOL // TILE) - 1).astype(jnp.int32)
    tile_cols = set_ends(jax.random.randint(key_of[3], (TILES,), 0, PIECE * N_BROW // TILE), jax.random.fold_in(key_of[3], 1), 0, (PIECE * N_BROW // TILE) - 1).astype(jnp.int32)
    counts = draw_counts(jax.random.fold_in(key_of[5], 71), 0)
    return {"vectors": vectors, "tiles": tiles, "tile_rows": tile_rows, "tile_cols": tile_cols, "counts": counts}


def reference(vectors, tiles, tile_rows, tile_cols, counts):
    lane = jnp.arange(TILE, dtype=jnp.int32)
    slot_ids = jnp.arange(TMAX, dtype=jnp.int32)
    source = vectors.astype(jnp.float32)

    def one_block(carry, index):
        brow_id = index // N_BCOL
        bcol_id = index % N_BCOL
        start = (index * TMAX).astype(jnp.int32)
        blocks = lax.dynamic_slice_in_dim(tiles, start, TMAX, 0).reshape(TMAX, TILE, TILE).astype(jnp.float32)
        rows_here = lax.dynamic_slice_in_dim(tile_rows, start, TMAX, 0)
        cols_here = lax.dynamic_slice_in_dim(tile_cols, start, TMAX, 0)
        live = (slot_ids < counts[brow_id, bcol_id]).astype(jnp.float32)
        global_rows = brow_id * N_BCOL * PIECE + rows_here[:, None] * TILE + lane[None, :]
        offset = cols_here[:, None] * TILE + lane[None, :]
        global_cols = ((offset // PIECE) * N_BCOL + bcol_id) * PIECE + offset % PIECE
        at_cols = source[:, global_cols]
        at_rows = source[:, global_rows]
        forward = jnp.einsum('ktj,tij->kti', at_cols, blocks, precision=lax.Precision.HIGHEST) * live[None, :, None]
        backward = jnp.einsum('kti,tij->ktj', at_rows, blocks, precision=lax.Precision.HIGHEST) * live[None, :, None]
        carry = carry.at[:, global_rows].add(forward)
        carry = carry.at[:, global_cols].add(backward)
        return carry, None

    start_sum = jnp.zeros(vectors.shape, jnp.float32)
    result, _ = lax.scan(one_block, start_sum, jnp.arange(N_BROW * N_BCOL, dtype=jnp.int32))
    return result
```

```python
import functools

import jax
import jax.numpy as jnp
from jax import lax
from jax.experimental import pallas as pl
from jax.experimental.pallas import tpu as pltpu
from jax.sharding import PartitionSpec as P

MESH = pl.DeviceIdType.MESH
TILE = 64
PIECE = 2048
SLOTS = 192
VECS = 8
NY, NX, NZH = 8, 4, 4
ROWS, COLS = 32, 16
GROUP = 16


def place():
    r = lax.axis_index("brow")
    c = lax.axis_index("bcol")
    return r, c, r // 16, (r // 2) % NY, r % 2, c // NX, c % NX


def row_id(zl, y, core):
    return zl * 16 + y * 2 + core


def remote(src, dst, send, recv, **where):
    return pltpu.make_async_remote_copy(
        src_ref=src, dst_ref=dst, send_sem=send, recv_sem=recv, device_id=where, device_id_type=MESH
    )


def greet(r, c, zl, y, core, zh, x):
    barrier = pltpu.get_barrier_semaphore()

    def call(**where):
        pl.semaphore_signal(barrier, inc=1, device_id=where, device_id_type=MESH)

    for d in (4, 3, 5, 2, 6, 1, 7):
        call(brow=row_id(zl, (y + d) % NY, core))
    for d in (2, 1, 3):
        call(bcol=((zh + d) % NZH) * NX + x)
    for d in (2, 1, 3):
        call(bcol=zh * NX + (x + d) % NX)
    call(brow=row_id(1 - zl, y, core))
    call(brow=row_id(zl, y, 1 - core))
    pl.semaphore_wait(barrier, 15)


def prep_kernel(tiles_ref, out_ref, flat, woven):
    lane = lax.broadcasted_iota(jnp.int32, (32, 128), 1)
    for b in range(32):
        flat[b * GROUP : (b + 1) * GROUP, :] = tiles_ref[:, b * 128 : (b + 1) * 128].astype(jnp.float32)
    for s in range(GROUP):
        m = flat[pl.ds(s, 32, stride=GROUP), :]
        turned = pltpu.roll(m, 64, 1)
        woven[pl.ds(s * TILE, 32, stride=2), :] = jnp.where(lane < 64, m, turned)
        woven[pl.ds(s * TILE + 1, 32, stride=2), :] = jnp.where(lane < 64, turned, m)
    for s in range(GROUP):
        out_ref[s] = woven[s * TILE : (s + 1) * TILE, :].astype(jnp.bfloat16)


def prep(tiles):
    return pl.pallas_call(
        prep_kernel,
        name="prep",
        grid=(SLOTS // GROUP,),
        in_specs=[pl.BlockSpec((GROUP, TILE * TILE), lambda g: (g, 0))],
        out_specs=pl.BlockSpec((GROUP, TILE, 128), lambda g: (g, 0, 0)),
        out_shape=jax.ShapeDtypeStruct((SLOTS, TILE, 128), jnp.bfloat16),
        scratch_shapes=[
            pltpu.VMEM((32 * GROUP, 128), jnp.float32),
            pltpu.VMEM((TILE * GROUP, 128), jnp.float32),
        ],
    )(tiles)


def gather_kernel(vec, col, row, col_send, col_recv, pass_send, near_send, row_send, row_recv, side_send, own_sem):
    r, c, zl, y, core, zh, x = place()
    z_mate = row_id(1 - zl, y, core)
    core_mate = row_id(zl, y, 1 - core)
    greet(r, c, zl, y, core, zh, x)
    sent = []

    def go(copy):
        copy.start()
        sent.append(copy)

    def arrived(buf, sems, index):
        remote(buf.at[index], buf.at[index], own_sem.at[0], sems.at[index], brow=core_mate).wait_recv()

    for n, d in enumerate((4, 3, 5, 2, 6, 1, 7)):
        go(remote(vec, col.at[r], col_send.at[n], col_recv.at[r], brow=row_id(zl, (y + d) % NY, core)))
    for n, d in enumerate((2, 1, 3)):
        go(remote(vec, row.at[c], row_send.at[n], row_recv.at[c], bcol=((zh + d) % NZH) * NX + x))
    go(remote(vec, col.at[r], pass_send.at[0], col_recv.at[r], brow=z_mate))
    for n, d in enumerate((2, 1, 3)):
        go(remote(vec, row.at[c], side_send.at[n], row_recv.at[c], bcol=zh * NX + (x + d) % NX))
    go(remote(vec, col.at[r], near_send.at[0], col_recv.at[r], brow=core_mate))
    mine = [
        pltpu.make_async_copy(vec, col.at[r], own_sem.at[1]),
        pltpu.make_async_copy(vec, row.at[c], own_sem.at[2]),
    ]
    for copy in mine:
        copy.start()

    def forward_y(n, d):
        src = row_id(zl, (y + d) % NY, core)
        arrived(col, col_recv, src)
        go(remote(col.at[src], col.at[src], pass_send.at[n], col_recv.at[src], brow=z_mate))
        go(remote(col.at[src], col.at[src], near_send.at[n], col_recv.at[src], brow=core_mate))

    def forward_zh(n, d):
        src = ((zh + d) % NZH) * NX + x
        arrived(row, row_recv, src)
        for m, e in enumerate((2, 1, 3)):
            go(
                remote(
                    row.at[src], row.at[src], side_send.at[3 * n + m], row_recv.at[src], bcol=zh * NX + (x + e) % NX
                )
            )

    def forward_z(n, d):
        src = row_id(1 - zl, (y + d) % NY, core)
        arrived(col, col_recv, src)
        go(remote(col.at[src], col.at[src], near_send.at[n], col_recv.at[src], brow=core_mate))

    forward_y(1, 1)
    forward_y(2, 7)
    forward_zh(1, 1)
    forward_zh(2, 3)
    forward_y(3, 2)
    forward_y(4, 6)
    forward_z(8, 0)
    forward_zh(3, 2)
    forward_y(5, 3)
    forward_y(6, 5)
    forward_z(9, 1)
    forward_z(10, 7)
    forward_y(7, 4)
    forward_z(11, 2)
    forward_z(12, 6)
    forward_z(13, 3)
    forward_z(14, 5)
    forward_z(15, 4)
    for copy in mine:
        copy.wait()
    for z in (0, 1):
        for d in range(NY):
            arrived(col, col_recv, row_id((zl + z) % 2, (y + d) % NY, 1 - core))
    for d in range(NZH):
        for e in (1, 2, 3):
            arrived(row, row_recv, ((zh + d) % NZH) * NX + (x + e) % NX)
    for copy in sent:
        copy.wait_send()


def gather(vectors):
    vmem = pl.BlockSpec(memory_space=pltpu.VMEM)
    dma = pltpu.SemaphoreType.DMA
    return pl.pallas_call(
        gather_kernel,
        name="gather",
        in_specs=[vmem],
        out_specs=[vmem, vmem],
        out_shape=[
            jax.ShapeDtypeStruct((ROWS, VECS, PIECE), jnp.bfloat16),
            jax.ShapeDtypeStruct((COLS, VECS, PIECE), jnp.bfloat16),
        ],
        scratch_shapes=[dma((7,)), dma((ROWS,)), dma((8,)), dma((16,)), dma((3,)), dma((COLS,)), dma((12,)), dma((3,))],
        compiler_params=pltpu.CompilerParams(collective_id=0, has_side_effects=True),
    )(vectors)


def apply_kernel(rows, cols, counts, tt, col, row, prow, pcol):
    n = counts[0, 0]
    prow[...] = jnp.zeros_like(prow)
    pcol[...] = jnp.zeros_like(pcol)
    high = (lax.broadcasted_iota(jnp.int32, (VECS, 128), 1) >= TILE).astype(jnp.int32)

    def spot(index):
        return index // 32, pl.ds(pl.multiple_of(((index // 2) % 16) * 128, 128), 128), index % 2

    def step(g, carry):
        done = []
        for u in range(8):
            s = g * 8 + u
            a, b = spot(rows[s]), spot(cols[s])
            live = (s < n).astype(jnp.int32)
            mask_a, mask_b = high == a[2], high == b[2]
            t = tt[s]
            w = jnp.concatenate([t, t], axis=0)
            xb = jnp.where(high == b[2] + 2 * (1 - live), col[b[0], :, b[1]].astype(jnp.float32), 0.0)
            xa = jnp.where(high == a[2] + 2 * (1 - live), row[a[0], :, a[1]].astype(jnp.float32), 0.0)
            fwd = lax.dot_general(
                xb.astype(jnp.bfloat16), w, (((1,), (1,)), ((), ())), preferred_element_type=jnp.float32
            )
            bwd = lax.dot_general(
                xa.astype(jnp.bfloat16), w, (((1,), (0,)), ((), ())), preferred_element_type=jnp.float32
            )
            done.append((a, b, jnp.where(mask_a, fwd, 0.0), jnp.where(mask_b, bwd, 0.0)))
        for a, b, fwd, bwd in done:
            prow[a[0], :, a[1]] += fwd
            pcol[b[0], :, b[1]] += bwd
        return carry

    lax.fori_loop(0, (n + 7) // 8, step, 0)


def apply(tile_rows, tile_cols, counts, tt, col, row):
    vmem = pl.BlockSpec(memory_space=pltpu.VMEM)
    smem = pl.BlockSpec(memory_space=pltpu.SMEM)
    return pl.pallas_call(
        apply_kernel,
        name="apply",
        in_specs=[smem, smem, smem, vmem, vmem, vmem],
        out_specs=[vmem, vmem],
        out_shape=[
            jax.ShapeDtypeStruct((COLS, VECS, PIECE), jnp.float32),
            jax.ShapeDtypeStruct((ROWS, VECS, PIECE), jnp.float32),
        ],
    )(tile_rows, tile_cols, counts, tt, col, row)


def scatter_kernel(
    prow, pcol, out, near_buf, near_sum, pass_buf, pass_sum, far_buf, side_buf, side_sum, hi_buf,
    near_send, near_recv, pass_send, pass_recv, far_send, far_recv, side_send, side_recv, hi_send, hi_recv,
):
    r, c, zl, y, core, zh, x = place()
    z_mate = row_id(1 - zl, y, core)
    core_mate = row_id(zl, y, 1 - core)
    greet(r, c, zl, y, core, zh, x)
    sent = []

    def go(copy):
        copy.start()
        sent.append(copy)

    def arrived(buf, sems, index):
        remote(buf.at[index], buf.at[index], near_send.at[0], sems.at[index], brow=core_mate).wait_recv()

    order = (4, 3, 5, 2, 6, 1, 7, 0)
    for z in (1, 0):
        for d in order:
            k = z * NY + d
            go(
                remote(
                    pcol.at[row_id((zl + z) % 2, (y + d) % NY, 1 - core)],
                    near_buf.at[k], near_send.at[k], near_recv.at[k], brow=core_mate,
                )
            )
    for d in (2, 1, 3, 0):
        for m, e in enumerate((2, 1, 3)):
            go(
                remote(
                    prow.at[((zh + d) % NZH) * NX + (x + e) % NX],
                    side_buf.at[3 * d + e - 1], side_send.at[3 * d + m], side_recv.at[3 * d + e - 1],
                    bcol=zh * NX + (x + e) % NX,
                )
            )
    for d in order:
        k = NY + d
        arrived(near_buf, near_recv, k)
        near_sum[k] = near_buf[k] + pcol[row_id(1 - zl, (y + d) % NY, core)]
        go(remote(near_sum.at[k], pass_buf.at[d], pass_send.at[d], pass_recv.at[d], brow=z_mate))
    for d in (2, 1, 3, 0):
        for e in (1, 3, 2):
            arrived(side_buf, side_recv, 3 * d + e - 1)
        total = prow[((zh + d) % NZH) * NX + x]
        for e in (1, 3, 2):
            total = total + side_buf[3 * d + e - 1]
        side_sum[d] = total
        if d:
            go(
                remote(
                    side_sum.at[d], hi_buf.at[d - 1], hi_send.at[d - 1], hi_recv.at[d - 1],
                    bcol=((zh + d) % NZH) * NX + x,
                )
            )
    for d in order:
        arrived(near_buf, near_recv, d)
        near_sum[d] = near_buf[d] + pcol[row_id(zl, (y + d) % NY, core)]
        arrived(pass_buf, pass_recv, d)
        pass_sum[d] = near_sum[d] + pass_buf[d]
        if d:
            go(
                remote(
                    pass_sum.at[d], far_buf.at[d - 1], far_send.at[d - 1], far_recv.at[d - 1],
                    brow=row_id(zl, (y + d) % NY, core),
                )
            )
    total = side_sum[0] + pass_sum[0]
    for d in (1, 3, 2):
        arrived(hi_buf, hi_recv, d - 1)
        total = total + hi_buf[d - 1]
    for d in (1, 7, 2, 6, 3, 5, 4):
        arrived(far_buf, far_recv, d - 1)
        total = total + far_buf[d - 1]
    out[...] = total
    for copy in sent:
        copy.wait_send()


def scatter(prow, pcol):
    vmem = pl.BlockSpec(memory_space=pltpu.VMEM)
    dma = pltpu.SemaphoreType.DMA

    def pieces(n):
        return pltpu.VMEM((n, VECS, PIECE), jnp.float32)

    return pl.pallas_call(
        scatter_kernel,
        name="scatter",
        in_specs=[vmem, vmem],
        out_specs=vmem,
        out_shape=jax.ShapeDtypeStruct((VECS, PIECE), jnp.float32),
        scratch_shapes=[pieces(16), pieces(16), pieces(8), pieces(8), pieces(7), pieces(12), pieces(4), pieces(3)]
        + [dma((n,)) for n in (16, 16, 8, 8, 7, 7, 12, 12, 3, 3)],
        compiler_params=pltpu.CompilerParams(collective_id=1, has_side_effects=True),
    )(prow, pcol)


def body(vectors, tiles, tile_rows, tile_cols, counts):
    tt = prep(tiles)
    col, row = gather(vectors)
    prow, pcol = apply(tile_rows, tile_cols, counts, tt, col, row)
    return scatter(prow, pcol)


def solution(mesh):
    return jax.shard_map(
        body,
        mesh=mesh,
        in_specs=(
            P(None, ("brow", "bcol")),
            P(("brow", "bcol"), None),
            P(("brow", "bcol")),
            P(("brow", "bcol")),
            P("brow", "bcol"),
        ),
        out_specs=P(None, ("brow", "bcol")),
        check_vma=False,
    )
```

```python
import functools

import jax
import jax.numpy as jnp
from jax import lax
from jax.experimental import pallas as pl
from jax.experimental.pallas import tpu as pltpu
from jax.sharding import PartitionSpec as P

MESH = pl.DeviceIdType.MESH
TILE = 64
PIECE = 2048
SLOTS = 192
VECS = 8
NY, NX, NZH = 8, 4, 4
ROWS, COLS = 32, 16
GROUP = 16
WIRE = PIECE + 128
FULL = 32000.0
VMEM = 16 << 20


def place():
    r = lax.axis_index("brow")
    c = lax.axis_index("bcol")
    return r, c, r // 16, (r // 2) % NY, r % 2, c // NX, c % NX


def row_id(zl, y, core):
    return zl * 16 + y * 2 + core


def remote(src, dst, send, recv, **where):
    return pltpu.make_async_remote_copy(
        src_ref=src, dst_ref=dst, send_sem=send, recv_sem=recv, device_id=where, device_id_type=MESH
    )


def greet(r, c, zl, y, core, zh, x):
    barrier = pltpu.get_barrier_semaphore()

    def call(**where):
        pl.semaphore_signal(barrier, inc=1, device_id=where, device_id_type=MESH)

    for d in (4, 3, 5, 2, 6, 1, 7):
        call(brow=row_id(zl, (y + d) % NY, core))
    for d in (2, 1, 3):
        call(bcol=((zh + d) % NZH) * NX + x)
    for d in (2, 1, 3):
        call(bcol=zh * NX + (x + d) % NX)
    call(brow=row_id(1 - zl, y, core))
    call(brow=row_id(zl, y, 1 - core))


def meet():
    pl.semaphore_wait(pltpu.get_barrier_semaphore(), 15)


def prep_group(g, tiles, out, flat, woven):
    lane = lax.broadcasted_iota(jnp.int32, (32, 128), 1)
    slots = pl.ds(pl.multiple_of(g * GROUP, GROUP), GROUP)
    for b in range(32):
        flat[b * GROUP : (b + 1) * GROUP, :] = tiles[slots, b * 128 : (b + 1) * 128].astype(jnp.float32)
    for s in range(GROUP):
        m = flat[pl.ds(s, 32, stride=GROUP), :]
        turned = pltpu.roll(m, 64, 1)
        woven[pl.ds(s * TILE, 32, stride=2), :] = jnp.where(lane < 64, m, turned)
        woven[pl.ds(s * TILE + 1, 32, stride=2), :] = jnp.where(lane < 64, turned, m)
    for s in range(GROUP):
        out[g * GROUP + s] = woven[s * TILE : (s + 1) * TILE, :].astype(jnp.bfloat16)


def gather_kernel(
    vec, tiles_hbm, col, row, tt, tiles, flat, woven,
    col_send, col_recv, pass_send, near_send, row_send, row_recv, side_send, own_sem, tile_sem,
):
    r, c, zl, y, core, zh, x = place()
    z_mate = row_id(1 - zl, y, core)
    core_mate = row_id(zl, y, 1 - core)
    halves = [
        pltpu.make_async_copy(tiles_hbm.at[pl.ds(h * 48, 48)], tiles.at[pl.ds(h * 48, 48)], tile_sem.at[h])
        for h in range(4)
    ]
    for copy in halves:
        copy.start()
    greet(r, c, zl, y, core, zh, x)
    sent = []

    def prep(lo, hi):
        def one(g, carry):
            prep_group(g, tiles, tt, flat, woven)
            return carry

        lax.fori_loop(lo, hi, one, 0)

    halves[0].wait()
    prep(0, 3)
    meet()

    def go(copy):
        copy.start()
        sent.append(copy)

    def arrived(buf, sems, index):
        remote(buf.at[index], buf.at[index], own_sem.at[0], sems.at[index], brow=core_mate).wait_recv()

    for n, d in enumerate((4, 3, 5, 2, 6, 1, 7)):
        go(remote(vec, col.at[r], col_send.at[n], col_recv.at[r], brow=row_id(zl, (y + d) % NY, core)))
    for n, d in enumerate((2, 1, 3)):
        go(remote(vec, row.at[c], row_send.at[n], row_recv.at[c], bcol=((zh + d) % NZH) * NX + x))
    go(remote(vec, col.at[r], pass_send.at[0], col_recv.at[r], brow=z_mate))
    for n, d in enumerate((2, 1, 3)):
        go(remote(vec, row.at[c], side_send.at[n], row_recv.at[c], bcol=zh * NX + (x + d) % NX))
    go(remote(vec, col.at[r], near_send.at[0], col_recv.at[r], brow=core_mate))
    mine = [
        pltpu.make_async_copy(vec, col.at[r], own_sem.at[1]),
        pltpu.make_async_copy(vec, row.at[c], own_sem.at[2]),
    ]
    for copy in mine:
        copy.start()
    halves[1].wait()
    prep(3, 5)

    def forward_y(n, d):
        src = row_id(zl, (y + d) % NY, core)
        arrived(col, col_recv, src)
        go(remote(col.at[src], col.at[src], pass_send.at[n], col_recv.at[src], brow=z_mate))
        go(remote(col.at[src], col.at[src], near_send.at[n], col_recv.at[src], brow=core_mate))

    def forward_zh(n, d):
        src = ((zh + d) % NZH) * NX + x
        arrived(row, row_recv, src)
        for m, e in enumerate((2, 1, 3)):
            go(
                remote(
                    row.at[src], row.at[src], side_send.at[3 * n + m], row_recv.at[src], bcol=zh * NX + (x + e) % NX
                )
            )

    def forward_z(n, d):
        src = row_id(1 - zl, (y + d) % NY, core)
        arrived(col, col_recv, src)
        go(remote(col.at[src], col.at[src], near_send.at[n], col_recv.at[src], brow=core_mate))

    forward_y(1, 1)
    forward_y(2, 7)
    forward_zh(1, 1)
    forward_zh(2, 3)
    prep(5, 6)
    forward_y(3, 2)
    forward_y(4, 6)
    forward_z(8, 0)
    forward_zh(3, 2)
    halves[2].wait()
    prep(6, 7)
    forward_y(5, 3)
    forward_y(6, 5)
    forward_z(9, 1)
    forward_z(10, 7)
    forward_y(7, 4)
    prep(7, 9)
    forward_z(11, 2)
    forward_z(12, 6)
    halves[3].wait()
    prep(9, 10)
    forward_z(13, 3)
    forward_z(14, 5)
    prep(10, 11)
    forward_z(15, 4)
    prep(11, 12)
    for copy in mine:
        copy.wait()
    for z in (0, 1):
        for d in range(NY):
            arrived(col, col_recv, row_id((zl + z) % 2, (y + d) % NY, 1 - core))
    for d in range(NZH):
        for e in (1, 2, 3):
            arrived(row, row_recv, ((zh + d) % NZH) * NX + (x + e) % NX)
    for copy in sent:
        copy.wait_send()


def gather(vectors, tiles):
    vmem = pl.BlockSpec(memory_space=pltpu.VMEM)
    dma = pltpu.SemaphoreType.DMA
    return pl.pallas_call(
        gather_kernel,
        name="gather",
        in_specs=[vmem, pl.BlockSpec(memory_space=pltpu.HBM)],
        out_specs=[vmem, vmem, vmem],
        out_shape=[
            jax.ShapeDtypeStruct((ROWS, VECS, PIECE), jnp.bfloat16),
            jax.ShapeDtypeStruct((COLS, VECS, PIECE), jnp.bfloat16),
            jax.ShapeDtypeStruct((SLOTS, TILE, 128), jnp.bfloat16),
        ],
        scratch_shapes=[
            pltpu.VMEM((SLOTS, TILE * TILE), jnp.bfloat16),
            pltpu.VMEM((32 * GROUP, 128), jnp.float32),
            pltpu.VMEM((TILE * GROUP, 128), jnp.float32),
        ]
        + [dma((n,)) for n in (7, ROWS, 8, 16, 3, COLS, 12, 3, 4)],
        compiler_params=pltpu.CompilerParams(collective_id=0, has_side_effects=True, vmem_limit_bytes=VMEM),
    )(vectors, tiles)


def apply_kernel(rows, cols, counts, tt, col, row, prow, pcol):
    n = counts[0, 0]
    prow[...] = jnp.zeros_like(prow)
    pcol[...] = jnp.zeros_like(pcol)
    high = (lax.broadcasted_iota(jnp.int32, (VECS, 128), 1) >= TILE).astype(jnp.int32)

    def spot(index):
        return index // 32, pl.ds(pl.multiple_of(((index // 2) % 16) * 128, 128), 128), index % 2

    def step(g, carry):
        done = []
        for u in range(8):
            s = g * 8 + u
            a, b = spot(rows[s]), spot(cols[s])
            live = (s < n).astype(jnp.int32)
            mask_a, mask_b = high == a[2], high == b[2]
            t = tt[s]
            w = jnp.concatenate([t, t], axis=0)
            xb = jnp.where(high == b[2] + 2 * (1 - live), col[b[0], :, b[1]].astype(jnp.float32), 0.0)
            xa = jnp.where(high == a[2] + 2 * (1 - live), row[a[0], :, a[1]].astype(jnp.float32), 0.0)
            fwd = lax.dot_general(
                xb.astype(jnp.bfloat16), w, (((1,), (1,)), ((), ())), preferred_element_type=jnp.float32
            )
            bwd = lax.dot_general(
                xa.astype(jnp.bfloat16), w, (((1,), (0,)), ((), ())), preferred_element_type=jnp.float32
            )
            done.append((a, b, jnp.where(mask_a, fwd, 0.0), jnp.where(mask_b, bwd, 0.0)))
        for a, b, fwd, bwd in done:
            prow[a[0], :, a[1]] += fwd
            pcol[b[0], :, b[1]] += bwd
        return carry

    lax.fori_loop(0, (n + 7) // 8, step, 0)


def apply(tile_rows, tile_cols, counts, tt, col, row):
    vmem = pl.BlockSpec(memory_space=pltpu.VMEM)
    smem = pl.BlockSpec(memory_space=pltpu.SMEM)
    return pl.pallas_call(
        apply_kernel,
        name="apply",
        in_specs=[smem, smem, smem, vmem, vmem, vmem],
        out_specs=[vmem, vmem],
        out_shape=[
            jax.ShapeDtypeStruct((COLS, VECS, PIECE), jnp.float32),
            jax.ShapeDtypeStruct((ROWS, VECS, PIECE), jnp.float32),
        ],
        compiler_params=pltpu.CompilerParams(vmem_limit_bytes=VMEM),
    )(tile_rows, tile_cols, counts, tt, col, row)


def blocks():
    return [slice(q * 128, (q + 1) * 128) for q in range(PIECE // 128)]


def pack(parts, wire):
    top = functools.reduce(jnp.maximum, [jnp.abs(p) for p in parts])
    power = jnp.floor(jnp.log2(jnp.maximum(top, 1e-30))) + 1.0
    scale = jnp.exp2(-power) * FULL
    for cut, p in zip(blocks(), parts):
        wire[:, cut] = jnp.round(p * scale).astype(jnp.int32).astype(jnp.int16)
    wire[:, PIECE:] = power.astype(jnp.int32).astype(jnp.int16)


def unpack(wire):
    def wide(cut):
        return wire[:, cut].astype(jnp.int32).astype(jnp.float32)

    scale = jnp.exp2(wide(slice(PIECE, WIRE))) * (1.0 / FULL)
    return [wide(cut) * scale for cut in blocks()]


def split(ref):
    return [ref[:, cut] for cut in blocks()]


def add(a, b):
    return [p + q for p, q in zip(a, b)]


def scatter_kernel(
    prow, pcol, out, near_buf, pass_out, pass_buf, far_out, far_buf, side_out, side_buf, hi_out, hi_buf,
    near_send, near_recv, pass_send, pass_recv, far_send, far_recv, side_send, side_recv, hi_send, hi_recv,
):
    r, c, zl, y, core, zh, x = place()
    z_mate = row_id(1 - zl, y, core)
    core_mate = row_id(zl, y, 1 - core)
    greet(r, c, zl, y, core, zh, x)
    sent = []

    def go(copy):
        copy.start()
        sent.append(copy)

    def arrived(buf, sems, index):
        remote(buf.at[index], buf.at[index], near_send.at[0], sems.at[index], brow=core_mate).wait_recv()

    def side_pack(d, e):
        k = 3 * d + e - 1
        pack(split(prow.at[((zh + d) % NZH) * NX + (x + e) % NX]), side_out.at[k])

    def side_go(d, e):
        k = 3 * d + e - 1
        go(remote(side_out.at[k], side_buf.at[k], side_send.at[k], side_recv.at[k], bcol=zh * NX + (x + e) % NX))

    for e in (2, 1, 3):
        side_pack(2, e)
    meet()
    order = (4, 3, 5, 2, 6, 1, 7, 0)
    for z in (1, 0):
        for d in order:
            k = z * NY + d
            go(
                remote(
                    pcol.at[row_id((zl + z) % 2, (y + d) % NY, 1 - core)],
                    near_buf.at[k], near_send.at[k], near_recv.at[k], brow=core_mate,
                )
            )
    for e in (2, 1, 3):
        side_go(2, e)

    def pass_on(d):
        k = NY + d
        arrived(near_buf, near_recv, k)
        pack(add(split(near_buf.at[k]), split(pcol.at[row_id(1 - zl, (y + d) % NY, core)])), pass_out.at[d])
        go(remote(pass_out.at[d], pass_buf.at[d], pass_send.at[d], pass_recv.at[d], brow=z_mate))

    def side_on(d):
        for e in (2, 1, 3):
            side_pack(d, e)
            side_go(d, e)

    def side_sum(d):
        total = split(prow.at[((zh + d) % NZH) * NX + x])
        for e in (1, 3, 2):
            arrived(side_buf, side_recv, 3 * d + e - 1)
            total = add(total, unpack(side_buf.at[3 * d + e - 1]))
        return total

    def hi_on(d):
        pack(side_sum(d), hi_out.at[d - 1])
        go(
            remote(
                hi_out.at[d - 1], hi_buf.at[d - 1], hi_send.at[d - 1], hi_recv.at[d - 1],
                bcol=((zh + d) % NZH) * NX + x,
            )
        )

    def far_sum(d):
        arrived(near_buf, near_recv, d)
        total = add(split(near_buf.at[d]), split(pcol.at[row_id(zl, (y + d) % NY, core)]))
        arrived(pass_buf, pass_recv, d)
        return add(total, unpack(pass_buf.at[d]))

    def far_on(d):
        pack(far_sum(d), far_out.at[d - 1])
        go(
            remote(
                far_out.at[d - 1], far_buf.at[d - 1], far_send.at[d - 1], far_recv.at[d - 1],
                brow=row_id(zl, (y + d) % NY, core),
            )
        )

    pass_on(4)
    side_on(1)
    pass_on(3)
    pass_on(5)
    side_on(3)
    pass_on(2)
    pass_on(6)
    side_on(0)
    far_on(4)
    hi_on(2)
    pass_on(1)
    pass_on(7)
    far_on(3)
    hi_on(1)
    pass_on(0)
    far_on(5)
    hi_on(3)
    for d in (2, 6, 1, 7):
        far_on(d)
    total = add(side_sum(0), far_sum(0))
    for d in (1, 3, 2):
        arrived(hi_buf, hi_recv, d - 1)
        total = add(total, unpack(hi_buf.at[d - 1]))
    for d in (1, 7, 2, 6, 3, 5, 4):
        arrived(far_buf, far_recv, d - 1)
        total = add(total, unpack(far_buf.at[d - 1]))
    for cut, p in zip(blocks(), total):
        out[:, cut] = p
    for copy in sent:
        copy.wait_send()


def scatter(prow, pcol):
    vmem = pl.BlockSpec(memory_space=pltpu.VMEM)
    dma = pltpu.SemaphoreType.DMA

    def wires(n):
        return pltpu.VMEM((n, VECS, WIRE), jnp.int16)

    return pl.pallas_call(
        scatter_kernel,
        name="scatter",
        in_specs=[vmem, vmem],
        out_specs=vmem,
        out_shape=jax.ShapeDtypeStruct((VECS, PIECE), jnp.float32),
        scratch_shapes=[pltpu.VMEM((16, VECS, PIECE), jnp.float32)]
        + [wires(n) for n in (8, 8, 7, 7, 12, 12, 3, 3)]
        + [dma((n,)) for n in (16, 16, 8, 8, 7, 7, 12, 12, 3, 3)],
        compiler_params=pltpu.CompilerParams(collective_id=1, has_side_effects=True, vmem_limit_bytes=VMEM),
    )(prow, pcol)


def body(vectors, tiles, tile_rows, tile_cols, counts):
    tiles, tile_rows, tile_cols = (
        pltpu.with_memory_space_constraint(a, pltpu.HBM) for a in (tiles, tile_rows, tile_cols)
    )
    col, row, tt = gather(vectors, tiles)
    prow, pcol = apply(tile_rows, tile_cols, counts, tt, col, row)
    return scatter(prow, pcol)


def solution(mesh):
    return jax.shard_map(
        body,
        mesh=mesh,
        in_specs=(
            P(None, ("brow", "bcol")),
            P(("brow", "bcol"), None),
            P(("brow", "bcol")),
            P(("brow", "bcol")),
            P("brow", "bcol"),
        ),
        out_specs=P(None, ("brow", "bcol")),
        check_vma=False,
    )
```

```python
import functools

import jax
import jax.numpy as jnp
from jax import lax
from jax.experimental import pallas as pl
from jax.experimental.pallas import tpu as pltpu
from jax.sharding import PartitionSpec as P

MESH = pl.DeviceIdType.MESH
TILE = 64
PIECE = 2048
SLOTS = 192
VECS = 8
NY, NX, NZH = 8, 4, 4
ROWS, COLS = 32, 16
GROUP = 16
UNROLL = 32
SPAN = 128
WIRE = PIECE + 128
FULL = 32000.0
VMEM = 32 << 20
BLOCKS = PIECE // 128


def place():
    r = lax.axis_index("brow")
    c = lax.axis_index("bcol")
    return r, c, r // 16, (r // 2) % NY, r % 2, c // NX, c % NX


def row_id(zl, y, core):
    return zl * 16 + y * 2 + core


def remote(src, dst, send, recv, **where):
    return pltpu.make_async_remote_copy(
        src_ref=src, dst_ref=dst, send_sem=send, recv_sem=recv, device_id=where, device_id_type=MESH
    )


def greet(zl, y, core, zh, x):
    barrier = pltpu.get_barrier_semaphore()

    def call(**where):
        pl.semaphore_signal(barrier, inc=1, device_id=where, device_id_type=MESH)

    for d in (2, 6, 1, 7):
        call(brow=row_id(zl, (y + d) % NY, core))
    for d in (2, 1, 3):
        call(bcol=((zh + d) % NZH) * NX + x)
        call(bcol=zh * NX + (x + d) % NX)
    call(brow=row_id(1 - zl, y, core))
    call(brow=row_id(zl, y, 1 - core))


def meet():
    pl.semaphore_wait(pltpu.get_barrier_semaphore(), 12)


def prep_group(g, tiles, out, flat, woven):
    lane = lax.broadcasted_iota(jnp.int32, (32, 128), 1)
    slots = pl.ds(pl.multiple_of(g * GROUP, GROUP), GROUP)
    for b in range(32):
        flat[b * GROUP : (b + 1) * GROUP, :] = tiles[slots, b * 128 : (b + 1) * 128].astype(jnp.float32)
    for s in range(GROUP):
        m = flat[pl.ds(s, 32, stride=GROUP), :]
        turned = pltpu.roll(m, 64, 1)
        woven[pl.ds(s * TILE, 32, stride=2), :] = jnp.where(lane < 64, m, turned)
        woven[pl.ds(s * TILE + 1, 32, stride=2), :] = jnp.where(lane < 64, turned, m)
    for s in range(GROUP):
        out[g * GROUP + s] = woven[s * TILE : (s + 1) * TILE, :].astype(jnp.bfloat16)


def blocks():
    return [slice(q * 128, (q + 1) * 128) for q in range(PIECE // 128)]


def pack(parts, wire):
    top = functools.reduce(jnp.maximum, [jnp.abs(p) for p in parts])
    power = jnp.floor(jnp.log2(jnp.maximum(top, 1e-30))) + 1.0
    scale = jnp.exp2(-power) * FULL
    for cut, p in zip(blocks(), parts):
        wire[:, cut] = jnp.round(p * scale).astype(jnp.int32).astype(jnp.int16)
    wire[:, PIECE:] = power.astype(jnp.int32).astype(jnp.int16)


def unpack(wire):
    def wide(cut):
        return wire[:, cut].astype(jnp.int32).astype(jnp.float32)

    scale = jnp.exp2(wide(slice(PIECE, WIRE))) * (1.0 / FULL)
    return [wide(cut) * scale for cut in blocks()]


def add(a, b):
    return [p + q for p, q in zip(a, b)]


def part(buf, piece):
    return buf.at[pl.ds(pl.multiple_of(piece * BLOCKS * VECS, BLOCKS * VECS), BLOCKS * VECS)]


def split(ref):
    return [ref[q * VECS : (q + 1) * VECS, :] for q in range(BLOCKS)]


def mark(hot, places):
    ids = places[...] >> 1
    ids = jnp.concatenate([ids, ids], axis=1)
    for block in range(hot.shape[0] // 64):
        spots = lax.broadcasted_iota(jnp.int32, (64, 2 * SLOTS), 0) + block * 64
        hot[block * 64 : (block + 1) * 64, :] = jnp.where(spots == ids, 1.0, 0.0).astype(jnp.bfloat16)


def products(to, at, counts, tt, seg, terms, forward):
    n = counts[0, 0]
    high = (lax.broadcasted_iota(jnp.int32, (VECS, 128), 1) >= TILE).astype(jnp.int32)

    def step(g, carry):
        for u in range(UNROLL):
            s = g * UNROLL + u
            dead = ((s >= n).astype(jnp.int32)) * 2
            given, wanted = at[s], to[s]
            own = jnp.where(high == (given & 1) + dead, seg[given >> 1].astype(jnp.float32), 0.0)
            if forward:
                half = lax.dot_general(
                    own.astype(jnp.bfloat16), tt[s], (((1,), (1,)), ((), ())), preferred_element_type=jnp.float32
                )
                both = jnp.concatenate([half, half], axis=1)
            else:
                own = (own + pltpu.roll(own, TILE, 1))[:, :TILE]
                both = jnp.dot(own.astype(jnp.bfloat16), tt[s], preferred_element_type=jnp.float32)
            terms[pl.ds(pl.multiple_of(s * VECS, VECS), VECS), :] = jnp.where(high == (wanted & 1), both, 0.0)
        return carry

    lax.fori_loop(0, SLOTS // UNROLL, step, 0)


def spread(terms, twins, hot, sums):
    for k in range(VECS):
        exact = terms[pl.ds(k, SLOTS, stride=VECS), :]
        top = exact.astype(jnp.bfloat16)
        twins[:SLOTS, k * 128 : (k + 1) * 128] = top
        twins[SLOTS:, k * 128 : (k + 1) * 128] = (exact - top.astype(jnp.float32)).astype(jnp.bfloat16)

    def step(block, carry):
        picks = hot[pl.ds(pl.multiple_of(block * SPAN, SPAN), SPAN), :]
        for k in range(0, VECS, 2):
            total = jnp.dot(picks, twins[:, k * 128 : (k + 2) * 128], preferred_element_type=jnp.float32)
            for m in (0, 1):
                sums[pl.ds(block * SPAN * VECS + k + m, SPAN, stride=VECS), :] = total[:, m * 128 : (m + 1) * 128]
        return carry

    lax.fori_loop(0, hot.shape[0] // SPAN, step, 0)


def kernel(
    cols, rows, counts, cols_vec, rows_vec, vec_hbm, tiles_hbm, out,
    vec, col, row, tiles, tt, flat, woven, pair_hot, side_hot, terms, twins, pcol, prow,
    near_buf, tree_out, tree_buf, more_out, more_buf, side_out, side_buf,
    near_send, tree_send, pass_send, col_recv, row_send, row_recv, own_sem, tile_sem, vec_sem,
    near_out, near_in, tree_from, tree_into, more_from, more_into, side_from, side_into,
):
    r, c, zl, y, core, zh, x = place()
    way = 1 - 2 * core
    halves = [
        pltpu.make_async_copy(tiles_hbm.at[pl.ds(h * 48, 48)], tiles.at[pl.ds(h * 48, 48)], tile_sem.at[h])
        for h in range(4)
    ]
    loads = [
        pltpu.make_async_copy(vec_hbm.at[:, cut], vec.at[q], vec_sem.at[q]) for q, cut in enumerate(blocks())
    ]
    for copy in loads:
        copy.start()
    greet(zl, y, core, zh, x)
    for copy in halves:
        copy.start()

    def prep(lo, hi):
        def one(g, carry):
            prep_group(g, tiles, tt, flat, woven)
            return carry

        lax.fori_loop(lo, hi, one, 0)

    for copy in loads:
        copy.wait()
    meet()

    def ahead(d, plane):
        return row_id(plane, (y + d + NY) % NY, core)

    def across(d, e):
        return ((zh + d + NZH) % NZH) * NX + (x + e + NX) % NX

    def hunk(buf, piece):
        return buf.at[pl.ds(piece * BLOCKS, BLOCKS)]

    def push_col(piece, sem, to, fresh=False):
        remote(vec if fresh else hunk(col, piece), hunk(col, piece), sem, col_recv.at[piece], brow=to).start()

    def push_row(piece, n, to, fresh=False):
        remote(vec if fresh else hunk(row, piece), hunk(row, piece), row_send.at[n], row_recv.at[piece], bcol=to).start()

    def got_col(piece):
        remote(hunk(col, piece), hunk(col, piece), own_sem.at[0], col_recv.at[piece], brow=r).wait_recv()

    def got_row(piece):
        remote(hunk(row, piece), hunk(row, piece), own_sem.at[0], row_recv.at[piece], bcol=c).wait_recv()

    z_mate = row_id(1 - zl, y, core)
    core_mate = row_id(zl, y, 1 - core)
    push_col(r, pass_send.at[0], z_mate, True)
    for n, d in enumerate((2, -2, 1, -1)):
        push_col(r, tree_send.at[n], ahead(d, zl), True)
    for n, d in enumerate((2, 1, -1)):
        push_row(c, n, across(d, 0), True)
    for n, d in enumerate((1, -1)):
        push_row(c, 3 + n, across(0, d), True)
    push_col(r, near_send.at[0], core_mate, True)
    mine = [
        pltpu.make_async_copy(vec, hunk(col, r), own_sem.at[1]),
        pltpu.make_async_copy(vec, hunk(row, c), own_sem.at[2]),
    ]
    for copy in mine:
        copy.start()
    halves[0].wait()
    prep(0, 3)
    halves[1].wait()
    prep(3, 5)
    mark(pair_hot, cols_vec)
    mark(side_hot, rows_vec)

    def near(n, piece):
        push_col(piece, near_send.at[n], core_mate)

    def branch(plane, way, sems, base, first):
        p = ahead(-2 * way, plane)
        got_col(p)
        push_col(p, sems.at[base], ahead(2 * way, plane))
        push_col(p, sems.at[base + 1], ahead(way, plane))
        near(first, p)
        q = ahead(2 * way, plane)
        got_col(q)
        push_col(q, sems.at[base + 2], ahead(-way, plane))
        near(first + 1, q)
        return p, q

    def side(n, d):
        p = across(d, 0)
        got_row(p)
        push_row(p, 3 + 2 * n, across(0, 1))
        push_row(p, 4 + 2 * n, across(0, -1))

    def far_side():
        p = across(2, 0)
        got_row(p)
        push_row(p, 14, across(0, 2))
        push_row(p, 9, across(0, 1))
        push_row(p, 10, across(0, -1))

    def round_side(n, d):
        p = across(d, -way)
        got_row(p)
        push_row(p, 11 + n, across(0, way))

    @pl.when(core == 0)
    def _():
        p, q = branch(zl, way, tree_send, 4, 1)
        push_col(p, pass_send.at[1], z_mate)
        push_col(q, pass_send.at[2], z_mate)
        side(1, -way)
        side(2, way)
        for n, d in ((3, 1), (4, -1)):
            p = ahead(d, zl)
            got_col(p)
            push_col(p, pass_send.at[n], z_mate)
            near(n, p)
        round_side(0, 0)
        halves[2].wait()
        prep(5, 7)
        far_side()
        for n, d in ((5, 3), (6, -3)):
            p = ahead(d, zl)
            got_col(p)
            push_col(p, pass_send.at[n], z_mate)
            near(n, p)
        round_side(1, -way)
        prep(7, 8)
        p = ahead(4, zl)
        got_col(p)
        push_col(p, pass_send.at[7], z_mate)
        near(7, p)
        round_side(2, way)
        prep(8, 9)
        for n, d in enumerate((0, 2, -2)):
            p = ahead(d, 1 - zl)
            got_col(p)
            near(8 + n, p)
        halves[3].wait()
        prep(9, 10)
        for n, d in enumerate((1, -1, 3, -3, 4)):
            p = ahead(d, 1 - zl)
            got_col(p)
            near(11 + n, p)

    @pl.when(core == 1)
    def _():
        p = ahead(0, 1 - zl)
        got_col(p)
        for n, d in enumerate((2, -2, 1, -1)):
            push_col(p, pass_send.at[1 + n], ahead(d, zl))
        near(1, p)
        branch(zl, way, tree_send, 4, 2)
        side(1, -way)
        side(2, way)
        for n, d in ((4, 1), (5, -1)):
            p = ahead(d, zl)
            got_col(p)
            near(n, p)
        round_side(0, 0)
        halves[2].wait()
        prep(5, 7)
        far_side()
        p = ahead(-2, 1 - zl)
        got_col(p)
        push_col(p, pass_send.at[5], ahead(2, zl))
        push_col(p, pass_send.at[6], ahead(1, zl))
        near(6, p)
        q = ahead(2, 1 - zl)
        got_col(q)
        push_col(q, pass_send.at[7], ahead(-1, zl))
        near(7, q)
        round_side(1, -way)
        prep(7, 8)
        for n, d in enumerate((3, -3, 4)):
            p = ahead(d, zl)
            got_col(p)
            near(8 + n, p)
        round_side(2, way)
        prep(8, 9)
        for n, d in enumerate((1, -1)):
            p = ahead(d, 1 - zl)
            got_col(p)
            near(11 + n, p)
        halves[3].wait()
        prep(9, 10)
        for n, d in enumerate((3, -3, 4)):
            p = ahead(d, 1 - zl)
            got_col(p)
            near(13 + n, p)

    prep(10, 12)
    for copy in mine:
        copy.wait()
    for d in range(NZH):
        got_row(across(d, way))
        got_row(across(d, 2))
    got_row(across(2, -way))
    products(cols, rows, counts, tt, row, terms, False)
    spread(terms, twins, pair_hot, pcol)

    def rel(d):
        return (d + NY) % NY

    def near_go(plane, d):
        k = plane * NY + rel(d)
        src = row_id((zl + plane) % 2, (y + d + NY) % NY, 1 - core)
        remote(part(pcol, src), near_buf.at[k], near_out.at[k], near_in.at[k], brow=core_mate).start()

    for d in (4, -3, 3, -2, 2, -1, 1, 0):
        near_go(1, d)
        near_go(0, d)
    for z in (0, 1):
        for d in range(NY):
            got_col(row_id((zl + z) % 2, (y + d) % NY, 1 - core))
    products(rows, cols, counts, tt, col, terms, True)
    spread(terms, twins, side_hot, prow)

    tree = (tree_out, tree_buf, tree_from, tree_into)
    more = (more_out, more_buf, more_from, more_into)
    side_kind = (side_out, side_buf, side_from, side_into)

    def send(kind, n, value, **to):
        held, buf, sends, recvs = kind
        pack(value, held.at[n])
        remote(held.at[n], buf.at[n], sends.at[n], recvs.at[n], **to).start()

    def take(kind, n, value):
        held, buf, _, recvs = kind
        remote(buf.at[n], buf.at[n], own_sem.at[0], recvs.at[n], brow=core_mate).wait_recv()
        return add(value, unpack(buf.at[n]))

    def pair(plane, d):
        k = plane * NY + rel(d)
        remote(near_buf.at[k], near_buf.at[k], own_sem.at[0], near_in.at[k], brow=core_mate).wait_recv()
        other = row_id((zl + plane) % 2, (y + d + NY) % NY, core)
        return add(split(near_buf.at[k]), split(part(pcol, other)))

    def own_row(d, e):
        return split(part(prow, across(d, e)))


    def outer(kind, way, value):
        send(kind, 1, value(-4 * way), brow=ahead(-2 * way, zl))
        send(kind, 0, value(-3 * way), brow=ahead(-way, zl))
        send(kind, 2, value(3 * way), brow=ahead(way, zl))

    def inner(kind, way, value):
        send(kind, 5, value(-way), brow=ahead(-way, zl))
        send(kind, 6, value(way), brow=ahead(way, zl))

    def middle(kind, way, value):
        send(kind, 4, take(kind, 2, value(2 * way)), brow=ahead(2 * way, zl))
        send(kind, 3, take(kind, 1, take(kind, 0, value(-2 * way))), brow=ahead(-2 * way, zl))

    def gathered(kind, value):
        for n in (5, 6, 4, 3):
            value = take(kind, n, value)
        return value

    def row_out_two(n, d):
        send(side_kind, 3 * n, own_row(d, 2), bcol=across(0, -way))
        send(side_kind, 3 * n + 1, own_row(d, way), bcol=across(0, way))

    def row_out_one(n, d):
        send(side_kind, 3 * n + 2, take(side_kind, 3 * n, own_row(d, -way)), bcol=across(0, -way))

    def row_sum(n, d):
        return take(side_kind, 3 * n + 2, take(side_kind, 3 * n + 1, own_row(d, 0)))

    def finish(total):
        for cut, p in zip(blocks(), total):
            out[:, cut] = p

    def row_total(total):
        total = add(total, row_sum(3, 0))
        for n in (13, 14, 12):
            total = take(side_kind, n, total)
        return total

    def row_far():
        send(side_kind, 0, own_row(2, 2), bcol=across(0, 2))
        send(side_kind, 1, own_row(2, way), bcol=across(0, way))
        send(side_kind, 2, own_row(2, -way), bcol=across(0, -way))

    def row_two():
        total = own_row(2, 0)
        for n in (2, 1, 0):
            total = take(side_kind, n, total)
        send(side_kind, 12, total, bcol=across(2, 0))

    def row_plus():
        send(side_kind, 13, row_sum(2, way), bcol=across(way, 0))

    def row_minus():
        send(side_kind, 14, row_sum(1, -way), bcol=across(-way, 0))

    @pl.when(core == 0)
    def _():

        def cross(d):
            send(more, rel(d), pair(1, d), brow=z_mate)

        def value(d):
            return take(more, rel(d), pair(0, d))

        row_out_two(1, -way)
        cross(4)
        cross(-3)
        cross(3)
        row_out_two(2, way)
        cross(-2)
        cross(2)
        row_far()
        cross(-1)
        cross(1)
        row_out_one(1, -way)
        cross(0)
        row_out_two(3, 0)
        outer(tree, way, value)
        row_out_one(2, way)
        row_two()
        row_minus()
        row_plus()
        middle(tree, way, value)
        row_out_one(3, 0)
        inner(tree, way, value)
        finish(row_total(gathered(tree, value(0))))

    @pl.when(core == 1)
    def _():

        def mine(d):
            return pair(0, d)

        def others(d):
            return pair(1, d)

        row_out_two(1, -way)
        outer(more, 1, others)
        row_out_two(2, way)
        outer(tree, way, mine)
        row_far()
        row_out_one(1, -way)
        row_out_two(3, 0)
        row_out_one(2, way)
        middle(more, 1, others)
        inner(more, 1, others)
        row_two()
        row_minus()
        row_plus()
        middle(tree, way, mine)
        inner(tree, way, mine)
        row_out_one(3, 0)
        send(more, 7, gathered(more, others(0)), brow=z_mate)
        finish(take(more, 7, row_total(gathered(tree, mine(0)))))

    for n in range(16):
        remote(part(pcol, 0), near_buf.at[0], near_out.at[n], own_sem.at[0], brow=core_mate).wait_send()
    for (held, buf, sends, recvs), count in ((tree, 7), (more, 8), (side_kind, 15)):
        for n in range(count):
            remote(held.at[n], buf.at[n], sends.at[n], own_sem.at[0], brow=core_mate).wait_send()
    for sems, count in ((near_send, 16), (tree_send, 7), (pass_send, 8)):
        for n in range(count):
            remote(vec, hunk(col, r), sems.at[n], own_sem.at[0], brow=core_mate).wait_send()
    for n in range(15):
        remote(vec, hunk(row, c), row_send.at[n], own_sem.at[0], bcol=c).wait_send()


def body(vectors, tiles, tile_rows, tile_cols, counts):
    vmem = pl.BlockSpec(memory_space=pltpu.VMEM)
    smem = pl.BlockSpec(memory_space=pltpu.SMEM)
    hbm = pl.BlockSpec(memory_space=pltpu.HBM)
    dma = pltpu.SemaphoreType.DMA
    bf16, f32 = jnp.bfloat16, jnp.float32

    def wires(n):
        return [pltpu.VMEM((n, VECS, WIRE), jnp.int16)] * 2

    def far(a):
        return pltpu.with_memory_space_constraint(a, pltpu.HBM)

    return pl.pallas_call(
        kernel,
        name="block_sparse",
        in_specs=[smem, smem, smem, vmem, vmem, hbm, hbm],
        out_specs=vmem,
        out_shape=jax.ShapeDtypeStruct((VECS, PIECE), f32),
        scratch_shapes=[
            pltpu.VMEM((BLOCKS, VECS, 128), bf16),
            pltpu.VMEM((ROWS * BLOCKS, VECS, 128), bf16),
            pltpu.VMEM((COLS * BLOCKS, VECS, 128), bf16),
            pltpu.VMEM((SLOTS, TILE * TILE), bf16),
            pltpu.VMEM((SLOTS, TILE, 128), bf16),
            pltpu.VMEM((32 * GROUP, 128), f32),
            pltpu.VMEM((TILE * GROUP, 128), f32),
            pltpu.VMEM((ROWS * BLOCKS, 2 * SLOTS), bf16),
            pltpu.VMEM((COLS * BLOCKS, 2 * SLOTS), bf16),
            pltpu.VMEM((SLOTS * VECS, 128), f32),
            pltpu.VMEM((2 * SLOTS, VECS * 128), bf16),
            pltpu.VMEM((ROWS * BLOCKS * VECS, 128), f32),
            pltpu.VMEM((COLS * BLOCKS * VECS, 128), f32),
            pltpu.VMEM((16, BLOCKS * VECS, 128), f32),
            *wires(7), *wires(8), *wires(15),
        ]
        + [dma((n,)) for n in (16, 7, 8, ROWS, 15, COLS, 3, 4, BLOCKS)]
        + [dma((n,)) for n in (16, 16, 7, 7, 8, 8, 15, 15)],
        compiler_params=pltpu.CompilerParams(collective_id=0, has_side_effects=True, vmem_limit_bytes=VMEM),
    )(
        far(tile_cols), far(tile_rows), counts, tile_cols.reshape(1, SLOTS), tile_rows.reshape(1, SLOTS),
        far(vectors), far(tiles),
    )


def solution(mesh):
    return jax.shard_map(
        body,
        mesh=mesh,
        in_specs=(
            P(None, ("brow", "bcol")),
            P(("brow", "bcol"), None),
            P(("brow", "bcol")),
            P(("brow", "bcol")),
            P("brow", "bcol"),
        ),
        out_specs=P(None, ("brow", "bcol")),
        check_vma=False,
    )
```

```python
import functools

import jax
import jax.numpy as jnp
from jax import lax
from jax.experimental import pallas as pl
from jax.experimental.pallas import tpu as pltpu
from jax.sharding import PartitionSpec as P

MESH = pl.DeviceIdType.MESH
TILE = 64
PIECE = 2048
SLOTS = 192
VECS = 8
NY, NX, NZH = 8, 4, 4
ROWS, COLS = 32, 16
GROUP = 16
UNROLL = 32
SPAN = 128
WIRE = PIECE + 128
FULL = 32000.0
VMEM = 32 << 20
BLOCKS = PIECE // 128


def place():
    r = lax.axis_index("brow")
    c = lax.axis_index("bcol")
    return r, c, r // 16, (r // 2) % NY, r % 2, c // NX, c % NX


def row_id(zl, y, core):
    return zl * 16 + y * 2 + core


def remote(src, dst, send, recv, **where):
    return pltpu.make_async_remote_copy(
        src_ref=src, dst_ref=dst, send_sem=send, recv_sem=recv, device_id=where, device_id_type=MESH
    )


def greet(zl, y, core, zh, x):
    barrier = pltpu.get_barrier_semaphore()

    def call(**where):
        pl.semaphore_signal(barrier, inc=1, device_id=where, device_id_type=MESH)

    for d in (2, 6, 1, 7):
        call(brow=row_id(zl, (y + d) % NY, core))
    for d in (2, 1, 3):
        call(bcol=((zh + d) % NZH) * NX + x)
        call(bcol=zh * NX + (x + d) % NX)
    call(brow=row_id(1 - zl, y, core))
    call(brow=row_id(zl, y, 1 - core))


def meet():
    pl.semaphore_wait(pltpu.get_barrier_semaphore(), 12)


def prep_group(g, tiles, out, flat, woven):
    lane = lax.broadcasted_iota(jnp.int32, (32, 128), 1)
    slots = pl.ds(pl.multiple_of(g * GROUP, GROUP), GROUP)
    for b in range(32):
        flat[b * GROUP : (b + 1) * GROUP, :] = tiles[slots, b * 128 : (b + 1) * 128].astype(jnp.float32)
    for s in range(GROUP):
        m = flat[pl.ds(s, 32, stride=GROUP), :]
        turned = pltpu.roll(m, 64, 1)
        woven[pl.ds(s * TILE, 32, stride=2), :] = jnp.where(lane < 64, m, turned)
        woven[pl.ds(s * TILE + 1, 32, stride=2), :] = jnp.where(lane < 64, turned, m)
    for s in range(GROUP):
        out[g * GROUP + s] = woven[s * TILE : (s + 1) * TILE, :].astype(jnp.bfloat16)


def blocks():
    return [slice(q * 128, (q + 1) * 128) for q in range(PIECE // 128)]


def pack(parts, wire):
    top = functools.reduce(jnp.maximum, [jnp.abs(p) for p in parts])
    power = jnp.floor(jnp.log2(jnp.maximum(top, 1e-30))) + 1.0
    scale = jnp.exp2(-power) * FULL
    for cut, p in zip(blocks(), parts):
        wire[:, cut] = jnp.round(p * scale).astype(jnp.int32).astype(jnp.int16)
    wire[:, PIECE:] = power.astype(jnp.int32).astype(jnp.int16)


def unpack(wire):
    def wide(cut):
        return wire[:, cut].astype(jnp.int32).astype(jnp.float32)

    scale = jnp.exp2(wide(slice(PIECE, WIRE))) * (1.0 / FULL)
    return [wide(cut) * scale for cut in blocks()]


def add(a, b):
    return [p + q for p, q in zip(a, b)]


def part(buf, piece):
    return buf.at[pl.ds(pl.multiple_of(piece * BLOCKS * VECS, BLOCKS * VECS), BLOCKS * VECS)]


def split(ref):
    return [ref[q * VECS : (q + 1) * VECS, :] for q in range(BLOCKS)]


def mark(hot, places):
    ids = places[...] >> 1
    ids = jnp.concatenate([ids, ids], axis=1)
    for block in range(hot.shape[0] // 64):
        spots = lax.broadcasted_iota(jnp.int32, (64, 2 * SLOTS), 0) + block * 64
        hot[block * 64 : (block + 1) * 64, :] = jnp.where(spots == ids, 1.0, 0.0).astype(jnp.bfloat16)


def products(g, to, at, counts, tt, seg, terms, forward):
    n = counts[0, 0]
    high = (lax.broadcasted_iota(jnp.int32, (VECS, 128), 1) >= TILE).astype(jnp.int32)

    for u in range(UNROLL):
        s = g * UNROLL + u
        dead = ((s >= n).astype(jnp.int32)) * 2
        given, wanted = at[s], to[s]
        own = jnp.where(high == (given & 1) + dead, seg[given >> 1].astype(jnp.float32), 0.0)
        if forward:
            half = lax.dot_general(
                own.astype(jnp.bfloat16), tt[s], (((1,), (1,)), ((), ())), preferred_element_type=jnp.float32
            )
            both = jnp.concatenate([half, half], axis=1)
        else:
            own = (own + pltpu.roll(own, TILE, 1))[:, :TILE]
            both = jnp.dot(own.astype(jnp.bfloat16), tt[s], preferred_element_type=jnp.float32)
        terms[s * VECS : (s + 1) * VECS, :] = jnp.where(high == (wanted & 1), both, 0.0)


def spread(terms, twins, hot, sums):
    for k in range(VECS):
        exact = terms[pl.ds(k, SLOTS, stride=VECS), :]
        top = exact.astype(jnp.bfloat16)
        twins[:SLOTS, k * 128 : (k + 1) * 128] = top
        twins[SLOTS:, k * 128 : (k + 1) * 128] = (exact - top.astype(jnp.float32)).astype(jnp.bfloat16)

    def step(block, carry):
        picks = hot[pl.ds(pl.multiple_of(block * SPAN, SPAN), SPAN), :]
        for k in range(0, VECS, 2):
            total = jnp.dot(picks, twins[:, k * 128 : (k + 2) * 128], preferred_element_type=jnp.float32)
            for m in (0, 1):
                sums[pl.ds(block * SPAN * VECS + k + m, SPAN, stride=VECS), :] = total[:, m * 128 : (m + 1) * 128]
        return carry

    lax.fori_loop(0, hot.shape[0] // SPAN, step, 0)


def kernel(
    cols_hbm, rows_hbm, counts, cols_flat, rows_flat, vec_hbm, tiles_hbm, out,
    cols, rows, cols_vec, rows_vec, vec, col, row, tiles, tt, flat, woven, pair_hot, side_hot, terms, twins, pcol, prow,
    near_buf, tree_out, tree_buf, more_out, more_buf, side_out, side_buf,
    near_send, tree_send, pass_send, col_recv, row_send, row_recv, own_sem, tile_sem, vec_sem, index_sem,
    near_out, near_in, tree_from, tree_into, more_from, more_into, side_from, side_into,
):
    r, c, zl, y, core, zh, x = place()
    way = 1 - 2 * core
    halves = [
        pltpu.make_async_copy(tiles_hbm.at[pl.ds(h * 48, 48)], tiles.at[pl.ds(h * 48, 48)], tile_sem.at[h])
        for h in range(4)
    ]
    loads = [
        pltpu.make_async_copy(vec_hbm.at[:, cut], vec.at[q], vec_sem.at[q]) for q, cut in enumerate(blocks())
    ]
    for copy in loads:
        copy.start()
    greet(zl, y, core, zh, x)
    for copy in halves:
        copy.start()
    lists = [
        pltpu.make_async_copy(a, b, index_sem.at[n])
        for n, (a, b) in enumerate(((cols_flat, cols_vec), (rows_flat, rows_vec), (cols_hbm, cols), (rows_hbm, rows)))
    ]
    for copy in lists:
        copy.start()

    def prep(lo, hi):
        def one(g, carry):
            prep_group(g, tiles, tt, flat, woven)
            return carry

        lax.fori_loop(lo, hi, one, 0)

    for copy in loads:
        copy.wait()
    meet()

    def ahead(d, plane):
        return row_id(plane, (y + d + NY) % NY, core)

    def across(d, e):
        return ((zh + d + NZH) % NZH) * NX + (x + e + NX) % NX

    def hunk(buf, piece):
        return buf.at[pl.ds(piece * BLOCKS, BLOCKS)]

    def push_col(piece, sem, to, fresh=False):
        remote(vec if fresh else hunk(col, piece), hunk(col, piece), sem, col_recv.at[piece], brow=to).start()

    def push_row(piece, n, to, fresh=False):
        remote(vec if fresh else hunk(row, piece), hunk(row, piece), row_send.at[n], row_recv.at[piece], bcol=to).start()

    def got_col(piece):
        remote(hunk(col, piece), hunk(col, piece), own_sem.at[0], col_recv.at[piece], brow=r).wait_recv()

    def got_row(piece):
        remote(hunk(row, piece), hunk(row, piece), own_sem.at[0], row_recv.at[piece], bcol=c).wait_recv()

    z_mate = row_id(1 - zl, y, core)
    core_mate = row_id(zl, y, 1 - core)
    push_col(r, pass_send.at[0], z_mate, True)
    for n, d in enumerate((2, -2, 1, -1)):
        push_col(r, tree_send.at[n], ahead(d, zl), True)
    for n, d in enumerate((2, 1, -1)):
        push_row(c, n, across(d, 0), True)
    for n, d in enumerate((1, -1)):
        push_row(c, 3 + n, across(0, d), True)
    push_col(r, near_send.at[0], core_mate, True)
    mine = [
        pltpu.make_async_copy(vec, hunk(col, r), own_sem.at[1]),
        pltpu.make_async_copy(vec, hunk(row, c), own_sem.at[2]),
    ]
    for copy in mine:
        copy.start()
    for h in range(3):
        halves[h].wait()
        prep(3 * h, 3 * h + 3)
    for copy in lists:
        copy.wait()
    mark(pair_hot, cols_vec)
    mark(side_hot, rows_vec)

    def near(n, piece):
        push_col(piece, near_send.at[n], core_mate)

    def branch(plane, way, sems, base, first):
        p = ahead(-2 * way, plane)
        got_col(p)
        push_col(p, sems.at[base], ahead(2 * way, plane))
        push_col(p, sems.at[base + 1], ahead(way, plane))
        near(first, p)
        q = ahead(2 * way, plane)
        got_col(q)
        push_col(q, sems.at[base + 2], ahead(-way, plane))
        near(first + 1, q)
        return p, q

    def side(n, d):
        p = across(d, 0)
        got_row(p)
        push_row(p, 3 + 2 * n, across(0, 1))
        push_row(p, 4 + 2 * n, across(0, -1))

    def far_side():
        p = across(2, 0)
        got_row(p)
        push_row(p, 14, across(0, 2))
        push_row(p, 9, across(0, 1))
        push_row(p, 10, across(0, -1))

    def round_side(n, d):
        p = across(d, -way)
        got_row(p)
        push_row(p, 11 + n, across(0, way))

    @pl.when(core == 0)
    def _():
        p, q = branch(zl, way, tree_send, 4, 1)
        push_col(p, pass_send.at[1], z_mate)
        push_col(q, pass_send.at[2], z_mate)
        side(1, -way)
        side(2, way)
        for n, d in ((3, 1), (4, -1)):
            p = ahead(d, zl)
            got_col(p)
            push_col(p, pass_send.at[n], z_mate)
            near(n, p)
        round_side(0, 0)
        halves[3].wait()
        prep(9, 10)
        far_side()
        for n, d in ((5, 3), (6, -3)):
            p = ahead(d, zl)
            got_col(p)
            push_col(p, pass_send.at[n], z_mate)
            near(n, p)
        round_side(1, -way)
        prep(10, 11)
        p = ahead(4, zl)
        got_col(p)
        push_col(p, pass_send.at[7], z_mate)
        near(7, p)
        round_side(2, way)
        prep(11, 12)

    @pl.when(core == 1)
    def _():
        p = ahead(0, 1 - zl)
        got_col(p)
        for n, d in enumerate((2, -2, 1, -1)):
            push_col(p, pass_send.at[1 + n], ahead(d, zl))
        near(1, p)
        branch(zl, way, tree_send, 4, 2)
        side(1, -way)
        side(2, way)
        for n, d in ((4, 1), (5, -1)):
            p = ahead(d, zl)
            got_col(p)
            near(n, p)
        round_side(0, 0)
        halves[3].wait()
        prep(9, 10)
        far_side()
        p = ahead(-2, 1 - zl)
        got_col(p)
        push_col(p, pass_send.at[5], ahead(2, zl))
        push_col(p, pass_send.at[6], ahead(1, zl))
        near(6, p)
        q = ahead(2, 1 - zl)
        got_col(q)
        push_col(q, pass_send.at[7], ahead(-1, zl))
        near(7, q)
        round_side(1, -way)
        prep(10, 11)
        round_side(2, way)
        prep(11, 12)

    for copy in mine:
        copy.wait()
    for d in range(NZH):
        got_row(across(d, way))
        got_row(across(d, 2))
    got_row(across(2, -way))
    last = zip(((0, 1), (2, 1), (-2, 1), (1, 1), (-1, 1), (3, 1), (-3, 1), (4, 1)),
               ((3, 0), (-3, 0), (4, 0), (1, 1), (-1, 1), (3, 1), (-3, 1), (4, 1)))
    for n, ((d0, z0), (d1, z1)) in enumerate(last):
        p = ahead(d0 + core * (d1 - d0), (zl + z0 + core * (z1 - z0)) % 2)
        got_col(p)
        near(8 + n, p)
        if n < SLOTS // UNROLL:
            products(n, cols, rows, counts, tt, row, terms, False)
    spread(terms, twins, pair_hot, pcol)

    def rel(d):
        return (d + NY) % NY

    def near_go(plane, d):
        k = plane * NY + rel(d)
        src = row_id((zl + plane) % 2, (y + d + NY) % NY, 1 - core)
        remote(part(pcol, src), near_buf.at[k], near_out.at[k], near_in.at[k], brow=core_mate).start()

    for d in (4, -3, 3, -2, 2, -1, 1, 0):
        near_go(1, d)
        near_go(0, d)
    for z in (0, 1):
        for d in range(NY):
            got_col(row_id((zl + z) % 2, (y + d) % NY, 1 - core))
    for n in range(SLOTS // UNROLL):
        products(n, rows, cols, counts, tt, col, terms, True)

    tree = (tree_out, tree_buf, tree_from, tree_into)
    more = (more_out, more_buf, more_from, more_into)
    side_kind = (side_out, side_buf, side_from, side_into)

    def send(kind, n, value, **to):
        held, buf, sends, recvs = kind
        pack(value, held.at[n])
        remote(held.at[n], buf.at[n], sends.at[n], recvs.at[n], **to).start()

    def take(kind, n, value):
        held, buf, _, recvs = kind
        remote(buf.at[n], buf.at[n], own_sem.at[0], recvs.at[n], brow=core_mate).wait_recv()
        return add(value, unpack(buf.at[n]))

    def pair(plane, d):
        k = plane * NY + rel(d)
        remote(near_buf.at[k], near_buf.at[k], own_sem.at[0], near_in.at[k], brow=core_mate).wait_recv()
        other = row_id((zl + plane) % 2, (y + d + NY) % NY, core)
        return add(split(near_buf.at[k]), split(part(pcol, other)))

    def own_row(d, e):
        return split(part(prow, across(d, e)))


    def outer(kind, way, value):
        send(kind, 1, value(-4 * way), brow=ahead(-2 * way, zl))
        send(kind, 0, value(-3 * way), brow=ahead(-way, zl))
        send(kind, 2, value(3 * way), brow=ahead(way, zl))

    def inner(kind, way, value):
        send(kind, 5, value(-way), brow=ahead(-way, zl))
        send(kind, 6, value(way), brow=ahead(way, zl))

    def middle(kind, way, value):
        send(kind, 4, take(kind, 2, value(2 * way)), brow=ahead(2 * way, zl))
        send(kind, 3, take(kind, 1, take(kind, 0, value(-2 * way))), brow=ahead(-2 * way, zl))

    def gathered(kind, value):
        for n in (5, 6, 4, 3):
            value = take(kind, n, value)
        return value

    def row_out_two(n, d):
        send(side_kind, 3 * n, own_row(d, 2), bcol=across(0, -way))
        send(side_kind, 3 * n + 1, own_row(d, way), bcol=across(0, way))

    def row_out_one(n, d):
        send(side_kind, 3 * n + 2, take(side_kind, 3 * n, own_row(d, -way)), bcol=across(0, -way))

    def row_sum(n, d):
        return take(side_kind, 3 * n + 2, take(side_kind, 3 * n + 1, own_row(d, 0)))

    def finish(total):
        for cut, p in zip(blocks(), total):
            out[:, cut] = p

    def row_total(total):
        total = add(total, row_sum(3, 0))
        for n in (13, 14, 12):
            total = take(side_kind, n, total)
        return total

    def row_far():
        send(side_kind, 0, own_row(2, 2), bcol=across(0, 2))
        send(side_kind, 1, own_row(2, way), bcol=across(0, way))
        send(side_kind, 2, own_row(2, -way), bcol=across(0, -way))

    def row_two():
        total = own_row(2, 0)
        for n in (2, 1, 0):
            total = take(side_kind, n, total)
        send(side_kind, 12, total, bcol=across(2, 0))

    def row_plus():
        send(side_kind, 13, row_sum(2, way), bcol=across(way, 0))

    def row_minus():
        send(side_kind, 14, row_sum(1, -way), bcol=across(-way, 0))

    def mine_of(d):
        return pair(0, d)

    def others(d):
        return pair(1, d)

    def crossed(d):
        return take(more, rel(d), pair(0, d))

    @pl.when(core == 0)
    def _():
        for d in (4, -3, 3, -2, 2, -1, 1, 0):
            send(more, rel(d), pair(1, d), brow=z_mate)

    @pl.when(core == 1)
    def _():
        outer(more, 1, others)
        outer(tree, way, mine_of)

    spread(terms, twins, side_hot, prow)

    @pl.when(core == 0)
    def _():
        row_out_two(1, -way)
        row_out_two(2, way)
        outer(tree, way, crossed)
        row_far()
        row_out_two(3, 0)
        inner(tree, way, crossed)
        row_out_one(1, -way)
        row_out_one(2, way)
        row_two()
        middle(tree, way, crossed)
        row_minus()
        row_plus()
        row_out_one(3, 0)
        finish(row_total(gathered(tree, crossed(0))))

    @pl.when(core == 1)
    def _():
        row_out_two(1, -way)
        row_out_two(2, way)
        row_far()
        inner(more, 1, others)
        middle(more, 1, others)
        row_out_two(3, 0)
        row_out_one(1, -way)
        row_out_one(2, way)
        inner(tree, way, mine_of)
        middle(tree, way, mine_of)
        row_two()
        row_minus()
        row_plus()
        send(more, 7, gathered(more, others(0)), brow=z_mate)
        row_out_one(3, 0)
        finish(take(more, 7, row_total(gathered(tree, mine_of(0)))))

    for n in range(16):
        remote(part(pcol, 0), near_buf.at[0], near_out.at[n], own_sem.at[0], brow=core_mate).wait_send()
    for (held, buf, sends, recvs), count in ((tree, 7), (more, 8), (side_kind, 15)):
        for n in range(count):
            remote(held.at[n], buf.at[n], sends.at[n], own_sem.at[0], brow=core_mate).wait_send()
    for sems, count in ((near_send, 16), (tree_send, 7), (pass_send, 8)):
        for n in range(count):
            remote(vec, hunk(col, r), sems.at[n], own_sem.at[0], brow=core_mate).wait_send()
    for n in range(15):
        remote(vec, hunk(row, c), row_send.at[n], own_sem.at[0], bcol=c).wait_send()


def body(vectors, tiles, tile_rows, tile_cols, counts):
    vmem = pl.BlockSpec(memory_space=pltpu.VMEM)
    smem = pl.BlockSpec(memory_space=pltpu.SMEM)
    hbm = pl.BlockSpec(memory_space=pltpu.HBM)
    dma = pltpu.SemaphoreType.DMA
    bf16, f32 = jnp.bfloat16, jnp.float32

    def wires(n):
        return [pltpu.VMEM((n, VECS, WIRE), jnp.int16)] * 2

    def far(a):
        return pltpu.with_memory_space_constraint(a, pltpu.HBM)

    return pl.pallas_call(
        kernel,
        name="block_sparse",
        in_specs=[hbm, hbm, smem, hbm, hbm, hbm, hbm],
        out_specs=vmem,
        out_shape=jax.ShapeDtypeStruct((VECS, PIECE), f32),
        scratch_shapes=[
            pltpu.SMEM((SLOTS,), jnp.int32),
            pltpu.SMEM((SLOTS,), jnp.int32),
            pltpu.VMEM((1, SLOTS), jnp.int32),
            pltpu.VMEM((1, SLOTS), jnp.int32),
            pltpu.VMEM((BLOCKS, VECS, 128), bf16),
            pltpu.VMEM((ROWS * BLOCKS, VECS, 128), bf16),
            pltpu.VMEM((COLS * BLOCKS, VECS, 128), bf16),
            pltpu.VMEM((SLOTS, TILE * TILE), bf16),
            pltpu.VMEM((SLOTS, TILE, 128), bf16),
            pltpu.VMEM((32 * GROUP, 128), f32),
            pltpu.VMEM((TILE * GROUP, 128), f32),
            pltpu.VMEM((ROWS * BLOCKS, 2 * SLOTS), bf16),
            pltpu.VMEM((COLS * BLOCKS, 2 * SLOTS), bf16),
            pltpu.VMEM((SLOTS * VECS, 128), f32),
            pltpu.VMEM((2 * SLOTS, VECS * 128), bf16),
            pltpu.VMEM((ROWS * BLOCKS * VECS, 128), f32),
            pltpu.VMEM((COLS * BLOCKS * VECS, 128), f32),
            pltpu.VMEM((16, BLOCKS * VECS, 128), f32),
            *wires(7), *wires(8), *wires(15),
        ]
        + [dma((n,)) for n in (16, 7, 8, ROWS, 15, COLS, 3, 4, BLOCKS, 4)]
        + [dma((n,)) for n in (16, 16, 7, 7, 8, 8, 15, 15)],
        compiler_params=pltpu.CompilerParams(collective_id=0, has_side_effects=True, vmem_limit_bytes=VMEM),
    )(
        far(tile_cols), far(tile_rows), counts, far(tile_cols.reshape(1, SLOTS)), far(tile_rows.reshape(1, SLOTS)),
        far(vectors), far(tiles),
    )


def solution(mesh):
    return jax.shard_map(
        body,
        mesh=mesh,
        in_specs=(
            P(None, ("brow", "bcol")),
            P(("brow", "bcol"), None),
            P(("brow", "bcol")),
            P(("brow", "bcol")),
            P("brow", "bcol"),
        ),
        out_specs=P(None, ("brow", "bcol")),
        check_vma=False,
    )
```

```python
import functools

import jax
import jax.numpy as jnp
from jax import lax
from jax.experimental import pallas as pl
from jax.experimental.pallas import tpu as pltpu
from jax.sharding import PartitionSpec as P

MESH = pl.DeviceIdType.MESH
TILE = 64
PIECE = 2048
SLOTS = 192
VECS = 8
NY, NX, NZH = 8, 4, 4
ROWS, COLS = 32, 16
GROUP = 16
UNROLL = 64
SPAN = 256
WIRE = PIECE + 128
FULL = 32000.0
VMEM = 32 << 20
BLOCKS = PIECE // 128


def place():
    r = lax.axis_index("brow")
    c = lax.axis_index("bcol")
    return r, c, r // 16, (r // 2) % NY, r % 2, c // NX, c % NX


def row_id(zl, y, core):
    return zl * 16 + y * 2 + core


def remote(src, dst, send, recv, **where):
    return pltpu.make_async_remote_copy(
        src_ref=src, dst_ref=dst, send_sem=send, recv_sem=recv, device_id=where, device_id_type=MESH
    )


def greet(zl, y, core, zh, x):
    barrier = pltpu.get_barrier_semaphore()

    def call(**where):
        pl.semaphore_signal(barrier, inc=1, device_id=where, device_id_type=MESH)

    for d in (2, 6, 1, 7):
        call(brow=row_id(zl, (y + d) % NY, core))
    for d in (2, 1, 3):
        call(bcol=((zh + d) % NZH) * NX + x)
        call(bcol=zh * NX + (x + d) % NX)
    call(brow=row_id(1 - zl, y, core))
    call(brow=row_id(zl, y, 1 - core))


def meet():
    pl.semaphore_wait(pltpu.get_barrier_semaphore(), 12)


def prep_group(g, tiles, out, flat, woven):
    lane = lax.broadcasted_iota(jnp.int32, (32, 128), 1)
    slots = pl.ds(pl.multiple_of(g * GROUP, GROUP), GROUP)
    for b in range(32):
        flat[b * GROUP : (b + 1) * GROUP, :] = tiles[slots, b * 128 : (b + 1) * 128].astype(jnp.float32)
    for s in range(GROUP):
        m = flat[pl.ds(s, 32, stride=GROUP), :]
        turned = pltpu.roll(m, 64, 1)
        woven[pl.ds(s * TILE, 32, stride=2), :] = jnp.where(lane < 64, m, turned)
        woven[pl.ds(s * TILE + 1, 32, stride=2), :] = jnp.where(lane < 64, turned, m)
    for s in range(GROUP):
        out[g * GROUP + s] = woven[s * TILE : (s + 1) * TILE, :].astype(jnp.bfloat16)


def blocks():
    return [slice(q * 128, (q + 1) * 128) for q in range(PIECE // 128)]


def pack(parts, wire):
    top = functools.reduce(jnp.maximum, [jnp.abs(p) for p in parts])
    power = jnp.floor(jnp.log2(jnp.maximum(top, 1e-30))) + 1.0
    scale = jnp.exp2(-power) * FULL
    for cut, p in zip(blocks(), parts):
        wire[:, cut] = jnp.round(p * scale).astype(jnp.int32).astype(jnp.int16)
    wire[:, PIECE:] = power.astype(jnp.int32).astype(jnp.int16)


def unpack(wire):
    def wide(cut):
        return wire[:, cut].astype(jnp.int32).astype(jnp.float32)

    scale = jnp.exp2(wide(slice(PIECE, WIRE))) * (1.0 / FULL)
    return [wide(cut) * scale for cut in blocks()]


def add(a, b):
    return [p + q for p, q in zip(a, b)]


def part(buf, piece):
    return buf.at[pl.ds(pl.multiple_of(piece * BLOCKS * VECS, BLOCKS * VECS), BLOCKS * VECS)]


def split(ref):
    return [ref[q * VECS : (q + 1) * VECS, :] for q in range(BLOCKS)]


def mark(hot, places):
    ids = places[...] >> 1
    ids = jnp.concatenate([ids, ids], axis=1)
    for block in range(hot.shape[0] // 64):
        spots = lax.broadcasted_iota(jnp.int32, (64, 2 * SLOTS), 0) + block * 64
        hot[block * 64 : (block + 1) * 64, :] = jnp.where(spots == ids, 1.0, 0.0).astype(jnp.bfloat16)


def products(g, to, at, counts, tt, seg, terms, forward):
    n = counts[0, 0]
    high = (lax.broadcasted_iota(jnp.int32, (VECS, 128), 1) >= TILE).astype(jnp.int32)

    for u in range(UNROLL):
        s = g * UNROLL + u
        dead = ((s >= n).astype(jnp.int32)) * 2
        given, wanted = at[s], to[s]
        own = jnp.where(high == (given & 1) + dead, seg[given >> 1].astype(jnp.float32), 0.0)
        if forward:
            half = lax.dot_general(
                own.astype(jnp.bfloat16), tt[s], (((1,), (1,)), ((), ())), preferred_element_type=jnp.float32
            )
            both = jnp.concatenate([half, half], axis=1)
        else:
            own = (own + pltpu.roll(own, TILE, 1))[:, :TILE]
            both = jnp.dot(own.astype(jnp.bfloat16), tt[s], preferred_element_type=jnp.float32)
        terms[s * VECS : (s + 1) * VECS, :] = jnp.where(high == (wanted & 1), both, 0.0)


def spread(terms, twins, hot, sums):
    for k in range(VECS):
        exact = terms[pl.ds(k, SLOTS, stride=VECS), :]
        top = exact.astype(jnp.bfloat16)
        twins[:SLOTS, k * 128 : (k + 1) * 128] = top
        twins[SLOTS:, k * 128 : (k + 1) * 128] = (exact - top.astype(jnp.float32)).astype(jnp.bfloat16)

    def step(block, carry):
        picks = hot[pl.ds(pl.multiple_of(block * SPAN, SPAN), SPAN), :]
        for k in range(0, VECS, 2):
            total = jnp.dot(picks, twins[:, k * 128 : (k + 2) * 128], preferred_element_type=jnp.float32)
            for m in (0, 1):
                sums[pl.ds(block * SPAN * VECS + k + m, SPAN, stride=VECS), :] = total[:, m * 128 : (m + 1) * 128]
        return carry

    lax.fori_loop(0, hot.shape[0] // SPAN, step, 0)


def kernel(
    cols_hbm, rows_hbm, counts, cols_flat, rows_flat, vec_hbm, tiles_hbm, out,
    cols, rows, cols_vec, rows_vec, vec, col, row, tiles, tt, flat, woven, pair_hot, side_hot, terms, twins, pcol, prow,
    near_buf, tree_out, tree_buf, more_out, more_buf, side_out, side_buf,
    near_send, tree_send, pass_send, col_recv, row_send, row_recv, own_sem, tile_sem, vec_sem, index_sem,
    near_out, near_in, tree_from, tree_into, more_from, more_into, side_from, side_into,
):
    r, c, zl, y, core, zh, x = place()
    way = 1 - 2 * core
    halves = [
        pltpu.make_async_copy(tiles_hbm.at[pl.ds(h * 48, 48)], tiles.at[pl.ds(h * 48, 48)], tile_sem.at[h])
        for h in range(4)
    ]
    loads = [
        pltpu.make_async_copy(vec_hbm.at[:, cut], vec.at[q], vec_sem.at[q]) for q, cut in enumerate(blocks())
    ]
    for copy in loads:
        copy.start()
    greet(zl, y, core, zh, x)
    for copy in halves:
        copy.start()
    lists = [
        pltpu.make_async_copy(a, b, index_sem.at[n])
        for n, (a, b) in enumerate(((cols_flat, cols_vec), (rows_flat, rows_vec), (cols_hbm, cols), (rows_hbm, rows)))
    ]
    for copy in lists:
        copy.start()

    def prep(lo, hi):
        def one(g, carry):
            prep_group(g, tiles, tt, flat, woven)
            return carry

        lax.fori_loop(lo, hi, one, 0)

    for copy in loads:
        copy.wait()
    meet()

    def ahead(d, plane):
        return row_id(plane, (y + d + NY) % NY, core)

    def across(d, e):
        return ((zh + d + NZH) % NZH) * NX + (x + e + NX) % NX

    def hunk(buf, piece):
        return buf.at[pl.ds(piece * BLOCKS, BLOCKS)]

    def push_col(piece, sem, to, fresh=False):
        remote(vec if fresh else hunk(col, piece), hunk(col, piece), sem, col_recv.at[piece], brow=to).start()

    def push_row(piece, n, to, fresh=False):
        remote(vec if fresh else hunk(row, piece), hunk(row, piece), row_send.at[n], row_recv.at[piece], bcol=to).start()

    def got_col(piece):
        remote(hunk(col, piece), hunk(col, piece), own_sem.at[0], col_recv.at[piece], brow=r).wait_recv()

    def got_row(piece):
        remote(hunk(row, piece), hunk(row, piece), own_sem.at[0], row_recv.at[piece], bcol=c).wait_recv()

    z_mate = row_id(1 - zl, y, core)
    core_mate = row_id(zl, y, 1 - core)
    push_col(r, pass_send.at[0], z_mate, True)
    for n, d in enumerate((2, -2, 1, -1)):
        push_col(r, tree_send.at[n], ahead(d, zl), True)
    for n, d in enumerate((2, 1, -1)):
        push_row(c, n, across(d, 0), True)
    for n, d in enumerate((1, -1)):
        push_row(c, 3 + n, across(0, d), True)
    push_col(r, near_send.at[0], core_mate, True)
    mine = [
        pltpu.make_async_copy(vec, hunk(col, r), own_sem.at[1]),
        pltpu.make_async_copy(vec, hunk(row, c), own_sem.at[2]),
    ]
    for copy in mine:
        copy.start()
    for h in range(3):
        halves[h].wait()
        prep(3 * h, 3 * h + 3)
    for copy in lists:
        copy.wait()
    mark(pair_hot, cols_vec)
    mark(side_hot, rows_vec)

    def near(n, piece):
        push_col(piece, near_send.at[n], core_mate)

    def branch(plane, way, sems, base, first):
        p = ahead(-2 * way, plane)
        got_col(p)
        push_col(p, sems.at[base], ahead(2 * way, plane))
        push_col(p, sems.at[base + 1], ahead(way, plane))
        near(first, p)
        q = ahead(2 * way, plane)
        got_col(q)
        push_col(q, sems.at[base + 2], ahead(-way, plane))
        near(first + 1, q)
        return p, q

    def side(n, d):
        p = across(d, 0)
        got_row(p)
        push_row(p, 3 + 2 * n, across(0, 1))
        push_row(p, 4 + 2 * n, across(0, -1))

    def far_side():
        p = across(2, 0)
        got_row(p)
        push_row(p, 14, across(0, 2))
        push_row(p, 9, across(0, 1))
        push_row(p, 10, across(0, -1))

    def round_side(n, d):
        p = across(d, -way)
        got_row(p)
        push_row(p, 11 + n, across(0, way))

    @pl.when(core == 0)
    def _():
        p, q = branch(zl, way, tree_send, 4, 1)
        push_col(p, pass_send.at[1], z_mate)
        push_col(q, pass_send.at[2], z_mate)
        side(1, -way)
        side(2, way)
        for n, d in ((3, 1), (4, -1)):
            p = ahead(d, zl)
            got_col(p)
            push_col(p, pass_send.at[n], z_mate)
            near(n, p)
        round_side(0, 0)
        halves[3].wait()
        prep(9, 10)
        far_side()
        for n, d in ((5, 3), (6, -3)):
            p = ahead(d, zl)
            got_col(p)
            push_col(p, pass_send.at[n], z_mate)
            near(n, p)
        round_side(1, -way)
        prep(10, 11)
        p = ahead(4, zl)
        got_col(p)
        push_col(p, pass_send.at[7], z_mate)
        near(7, p)
        round_side(2, way)
        prep(11, 12)

    @pl.when(core == 1)
    def _():
        p = ahead(0, 1 - zl)
        got_col(p)
        for n, d in enumerate((2, -2, 1, -1)):
            push_col(p, pass_send.at[1 + n], ahead(d, zl))
        near(1, p)
        branch(zl, way, tree_send, 4, 2)
        side(1, -way)
        side(2, way)
        for n, d in ((4, 1), (5, -1)):
            p = ahead(d, zl)
            got_col(p)
            near(n, p)
        round_side(0, 0)
        halves[3].wait()
        prep(9, 10)
        far_side()
        p = ahead(-2, 1 - zl)
        got_col(p)
        push_col(p, pass_send.at[5], ahead(2, zl))
        push_col(p, pass_send.at[6], ahead(1, zl))
        near(6, p)
        q = ahead(2, 1 - zl)
        got_col(q)
        push_col(q, pass_send.at[7], ahead(-1, zl))
        near(7, q)
        round_side(1, -way)
        prep(10, 11)
        round_side(2, way)
        prep(11, 12)

    for copy in mine:
        copy.wait()
    for d in range(NZH):
        got_row(across(d, way))
        got_row(across(d, 2))
    got_row(across(2, -way))
    last = zip(((0, 1), (2, 1), (-2, 1), (1, 1), (-1, 1), (3, 1), (-3, 1), (4, 1)),
               ((3, 0), (-3, 0), (4, 0), (1, 1), (-1, 1), (3, 1), (-3, 1), (4, 1)))
    for n, ((d0, z0), (d1, z1)) in enumerate(last):
        p = ahead(d0 + core * (d1 - d0), (zl + z0 + core * (z1 - z0)) % 2)
        got_col(p)
        near(8 + n, p)
        if n < SLOTS // UNROLL:
            products(n, cols, rows, counts, tt, row, terms, False)
    spread(terms, twins, pair_hot, pcol)

    def rel(d):
        return (d + NY) % NY

    def near_go(plane, d):
        k = plane * NY + rel(d)
        src = row_id((zl + plane) % 2, (y + d + NY) % NY, 1 - core)
        remote(part(pcol, src), near_buf.at[k], near_out.at[k], near_in.at[k], brow=core_mate).start()

    for d in (4, -3, 3, -2, 2, -1, 1, 0):
        near_go(1, d)
        near_go(0, d)
    for z in (0, 1):
        for d in range(NY):
            got_col(row_id((zl + z) % 2, (y + d) % NY, 1 - core))
    for n in range(SLOTS // UNROLL):
        products(n, rows, cols, counts, tt, col, terms, True)

    tree = (tree_out, tree_buf, tree_from, tree_into)
    more = (more_out, more_buf, more_from, more_into)
    side_kind = (side_out, side_buf, side_from, side_into)

    def send(kind, n, value, **to):
        held, buf, sends, recvs = kind
        pack(value, held.at[n])
        remote(held.at[n], buf.at[n], sends.at[n], recvs.at[n], **to).start()

    def take(kind, n, value):
        held, buf, _, recvs = kind
        remote(buf.at[n], buf.at[n], own_sem.at[0], recvs.at[n], brow=core_mate).wait_recv()
        return add(value, unpack(buf.at[n]))

    def pair(plane, d):
        k = plane * NY + rel(d)
        remote(near_buf.at[k], near_buf.at[k], own_sem.at[0], near_in.at[k], brow=core_mate).wait_recv()
        other = row_id((zl + plane) % 2, (y + d + NY) % NY, core)
        return add(split(near_buf.at[k]), split(part(pcol, other)))

    def own_row(d, e):
        return split(part(prow, across(d, e)))


    def outer(kind, way, value):
        send(kind, 1, value(-4 * way), brow=ahead(-2 * way, zl))
        send(kind, 0, value(-3 * way), brow=ahead(-way, zl))
        send(kind, 2, value(3 * way), brow=ahead(way, zl))

    def inner(kind, way, value):
        send(kind, 5, value(-way), brow=ahead(-way, zl))
        send(kind, 6, value(way), brow=ahead(way, zl))

    def middle(kind, way, value):
        send(kind, 4, take(kind, 2, value(2 * way)), brow=ahead(2 * way, zl))
        send(kind, 3, take(kind, 1, take(kind, 0, value(-2 * way))), brow=ahead(-2 * way, zl))

    def gathered(kind, value):
        for n in (5, 6, 4, 3):
            value = take(kind, n, value)
        return value

    def row_out_two(n, d):
        send(side_kind, 3 * n, own_row(d, 2), bcol=across(0, -way))
        send(side_kind, 3 * n + 1, own_row(d, way), bcol=across(0, way))

    def row_out_one(n, d):
        send(side_kind, 3 * n + 2, take(side_kind, 3 * n, own_row(d, -way)), bcol=across(0, -way))

    def row_sum(n, d):
        return take(side_kind, 3 * n + 2, take(side_kind, 3 * n + 1, own_row(d, 0)))

    def finish(total):
        for cut, p in zip(blocks(), total):
            out[:, cut] = p

    def row_total(total):
        total = add(total, row_sum(3, 0))
        for n in (13, 14, 12):
            total = take(side_kind, n, total)
        return total

    def row_far():
        send(side_kind, 0, own_row(2, 2), bcol=across(0, 2))
        send(side_kind, 1, own_row(2, way), bcol=across(0, way))
        send(side_kind, 2, own_row(2, -way), bcol=across(0, -way))

    def row_two():
        total = own_row(2, 0)
        for n in (2, 1, 0):
            total = take(side_kind, n, total)
        send(side_kind, 12, total, bcol=across(2, 0))

    def row_plus():
        send(side_kind, 13, row_sum(2, way), bcol=across(way, 0))

    def row_minus():
        send(side_kind, 14, row_sum(1, -way), bcol=across(-way, 0))

    def mine_of(d):
        return pair(0, d)

    def others(d):
        return pair(1, d)

    def crossed(d):
        return take(more, rel(d), pair(0, d))

    @pl.when(core == 0)
    def _():
        for d in (4, -3, 3, -2, 2, -1, 1, 0):
            send(more, rel(d), pair(1, d), brow=z_mate)

    @pl.when(core == 1)
    def _():
        outer(more, 1, others)
        outer(tree, way, mine_of)

    spread(terms, twins, side_hot, prow)

    @pl.when(core == 0)
    def _():
        row_out_two(1, -way)
        row_out_two(2, way)
        outer(tree, way, crossed)
        row_far()
        row_out_two(3, 0)
        inner(tree, way, crossed)
        row_out_one(1, -way)
        row_out_one(2, way)
        row_two()
        middle(tree, way, crossed)
        row_minus()
        row_plus()
        row_out_one(3, 0)
        finish(row_total(gathered(tree, crossed(0))))

    @pl.when(core == 1)
    def _():
        row_out_two(1, -way)
        row_out_two(2, way)
        row_far()
        inner(more, 1, others)
        middle(more, 1, others)
        row_out_two(3, 0)
        row_out_one(1, -way)
        row_out_one(2, way)
        inner(tree, way, mine_of)
        middle(tree, way, mine_of)
        row_two()
        row_minus()
        row_plus()
        send(more, 7, gathered(more, others(0)), brow=z_mate)
        row_out_one(3, 0)
        finish(take(more, 7, row_total(gathered(tree, mine_of(0)))))

    for n in range(16):
        remote(part(pcol, 0), near_buf.at[0], near_out.at[n], own_sem.at[0], brow=core_mate).wait_send()
    for (held, buf, sends, recvs), count in ((tree, 7), (more, 8), (side_kind, 15)):
        for n in range(count):
            remote(held.at[n], buf.at[n], sends.at[n], own_sem.at[0], brow=core_mate).wait_send()
    for sems, count in ((near_send, 16), (tree_send, 7), (pass_send, 8)):
        for n in range(count):
            remote(vec, hunk(col, r), sems.at[n], own_sem.at[0], brow=core_mate).wait_send()
    for n in range(15):
        remote(vec, hunk(row, c), row_send.at[n], own_sem.at[0], bcol=c).wait_send()


def body(vectors, tiles, tile_rows, tile_cols, counts):
    vmem = pl.BlockSpec(memory_space=pltpu.VMEM)
    smem = pl.BlockSpec(memory_space=pltpu.SMEM)
    hbm = pl.BlockSpec(memory_space=pltpu.HBM)
    dma = pltpu.SemaphoreType.DMA
    bf16, f32 = jnp.bfloat16, jnp.float32

    def wires(n):
        return [pltpu.VMEM((n, VECS, WIRE), jnp.int16)] * 2

    def far(a):
        return pltpu.with_memory_space_constraint(a, pltpu.HBM)

    return pl.pallas_call(
        kernel,
        name="block_sparse",
        in_specs=[hbm, hbm, smem, hbm, hbm, hbm, hbm],
        out_specs=vmem,
        out_shape=jax.ShapeDtypeStruct((VECS, PIECE), f32),
        scratch_shapes=[
            pltpu.SMEM((SLOTS,), jnp.int32),
            pltpu.SMEM((SLOTS,), jnp.int32),
            pltpu.VMEM((1, SLOTS), jnp.int32),
            pltpu.VMEM((1, SLOTS), jnp.int32),
            pltpu.VMEM((BLOCKS, VECS, 128), bf16),
            pltpu.VMEM((ROWS * BLOCKS, VECS, 128), bf16),
            pltpu.VMEM((COLS * BLOCKS, VECS, 128), bf16),
            pltpu.VMEM((SLOTS, TILE * TILE), bf16),
            pltpu.VMEM((SLOTS, TILE, 128), bf16),
            pltpu.VMEM((32 * GROUP, 128), f32),
            pltpu.VMEM((TILE * GROUP, 128), f32),
            pltpu.VMEM((ROWS * BLOCKS, 2 * SLOTS), bf16),
            pltpu.VMEM((COLS * BLOCKS, 2 * SLOTS), bf16),
            pltpu.VMEM((SLOTS * VECS, 128), f32),
            pltpu.VMEM((2 * SLOTS, VECS * 128), bf16),
            pltpu.VMEM((ROWS * BLOCKS * VECS, 128), f32),
            pltpu.VMEM((COLS * BLOCKS * VECS, 128), f32),
            pltpu.VMEM((16, BLOCKS * VECS, 128), f32),
            *wires(7), *wires(8), *wires(15),
        ]
        + [dma((n,)) for n in (16, 7, 8, ROWS, 15, COLS, 3, 4, BLOCKS, 4)]
        + [dma((n,)) for n in (16, 16, 7, 7, 8, 8, 15, 15)],
        compiler_params=pltpu.CompilerParams(collective_id=0, has_side_effects=True, vmem_limit_bytes=VMEM),
    )(
        far(tile_cols), far(tile_rows), counts, far(tile_cols.reshape(1, SLOTS)), far(tile_rows.reshape(1, SLOTS)),
        far(vectors), far(tiles),
    )


def solution(mesh):
    return jax.shard_map(
        body,
        mesh=mesh,
        in_specs=(
            P(None, ("brow", "bcol")),
            P(("brow", "bcol"), None),
            P(("brow", "bcol")),
            P(("brow", "bcol")),
            P("brow", "bcol"),
        ),
        out_specs=P(None, ("brow", "bcol")),
        check_vma=False,
    )
```
